32 devices in a mesh: ctx: 8 (over z, x), head: 4 (over y, core).
Axes of the slice: x: 2, y: 2, z: 4, core: 2. Of those that a mesh axis runs over, the one named last changes fastest.
Arguments:
- x_in: bfloat16 [8192, 4096], P('ctx', 'head'), may hold values from -6 to 6
- b_in: bfloat16 [8192, 128], P('ctx'), may hold values from -1.796875 to 1.796875
- c_in: bfloat16 [8192, 128], P('ctx'), may hold values from -1.796875 to 1.796875
- d_out: bfloat16 [8192, 4096], P('ctx', 'head'), may hold values from -0.75 to 0.75
- table: float32 [16, 18], replicated, may hold values from 0 to 3, as said below
- level_index: int32 [8192], P('ctx'), may hold values from 0 to 15
Outputs:
- y_out: bfloat16 [8192, 4096], P('ctx', 'head')
- dx_out: bfloat16 [8192, 4096], P('ctx', 'head')
- d_b: float32 [8192, 128], P(('ctx', 'head'))
- d_c: float32 [8192, 128], P(('ctx', 'head'))
The draws below stay inside these ranges and needn't reach their ends.
Inputs may be any that keep to these rules, and one draw needn't show every extreme that they name: `table`: entries are positive.
All inputs are finite; a program needn't handle non-finite values.
Results may differ from the reference program's by a relative error of at most 0.006.
Values sent between devices are 32-bit elements; how exact they have to be, the bound alone decides.
A program may use at most 128 MiB of HBM per device.

```python
import jax
import jax.numpy as jnp
from jax import lax

HEADS = 64
HEAD_DIM = 64
NSTATE = 128
TOK_DEV = 1024
NTAB = 16
LEVELS = 18
TOKENS = 8192
WIDTH = 4096
N_CTX = 8
N_HEAD = 4


def draw_table(key, part):
    raw_draw = jax.random.uniform(key, (NTAB, LEVELS), jnp.float32)
    row_scale = jnp.exp(jnp.log(0.3) + raw_draw * jnp.log(10.0))
    falloff = jnp.exp2(-0.5 * jnp.arange(LEVELS, dtype=jnp.float32))
    return (row_scale * falloff[None, :]).astype(jnp.float32)


def set_ends(values, stream_key, smallest, high):
    longest = values.shape.index(max(values.shape))
    spots = []
    for shift in (0, 1):
        where = [jax.random.randint(jax.random.fold_in(stream_key, axis), (), 0, length) for axis, length in enumerate(values.shape)]
        where[longest] = (where[longest] + shift) % values.shape[longest]
        spots.append(tuple(where))
    return values.at[spots[0]].set(smallest).at[spots[1]].set(high)


def block_scale(rng, extent, split, low, high):
    loudness = 1.0
    for dim, shards_of in split:
        draws = jax.random.uniform(jax.random.fold_in(jax.random.fold_in(rng, 6), dim), (shards_of,), jnp.float32, low / len(split), high / len(split))
        loudness = loudness * jnp.repeat(jnp.exp(draws), extent[dim] // shards_of).reshape((-1,) + (1,) * (len(extent) - 1 - dim))
    return loudness


def normal_values(rng, extent, width, most, cuts=(), kind=jnp.bfloat16):
    loudness = block_scale(rng, extent, cuts, -0.22, 0.18) if cuts else 1.0
    values = jax.random.normal(rng, extent, jnp.float32) * width * loudness
    return jnp.minimum(jnp.maximum(values, -most), most).astype(kind)


def setup_inputs(seed: int = 0) -> dict:
    key_of = jax.random.split(jax.random.key(seed), 7)
    x_in = normal_values(key_of[0], (TOKENS, WIDTH), 1.0, 6.0, ((0, 8), (1, 4)))
    b_in = normal_values(key_of[1], (TOKENS, NSTATE), 0.3, 1.796875, ((0, 8),))
    c_in = normal_values(key_of[2], (TOKENS, NSTATE), 0.3, 1.796875, ((0, 8),))
    d_out = normal_values(key_of[3], (TOKENS, WIDTH), 0.125, 0.75, ((0, 8), (1, 4)))
    table = draw_table(jax.random.fold_in(key_of[6], 71), 0)
    level_index = set_ends(jax.random.randint(key_of[5], (TOKENS,), 0, NTAB), jax.random.fold_in(key_of[5], 1), 0, NTAB - 1).astype(jnp.int32)
    return dict(x_in=x_in, b_in=b_in, c_in=c_in, d_out=d_out, table=table, level_index=level_index)


def bit_count(values, bits):
    counted = jnp.zeros(values.shape, jnp.int32)
    for digit_no in range(bits):
        counted = counted + (values >= (1 << digit_no)).astype(jnp.int32)
    return counted


def reference(x_in, b_in, c_in, d_out, table, level_index):
    num_blocks = N_CTX
    tok_rows = TOK_DEV
    feat_width = HEADS * HEAD_DIM
    groups_head = N_HEAD
    ctx_bits = num_blocks.bit_length() - 1
    low_bits = tok_rows.bit_length() - 1
    weights_tok = table[level_index]
    xs_block = x_in.reshape(num_blocks, tok_rows, feat_width)
    bs_block = b_in.reshape(num_blocks, tok_rows, NSTATE)
    cs_block = c_in.reshape(num_blocks, tok_rows, NSTATE)
    ds_block = d_out.reshape(num_blocks, tok_rows, feat_width)
    lam_block = weights_tok.reshape(num_blocks, tok_rows, LEVELS)
    state = jnp.einsum("cln,clp->cnp", bs_block.astype(jnp.float32), xs_block.astype(jnp.float32))
    block_ids = jnp.arange(num_blocks, dtype=jnp.int32)
    top_bit = bit_count(block_ids[:, None] ^ block_ids[None, :], ctx_bits) - 1
    level_ids = jnp.arange(ctx_bits, dtype=jnp.int32)
    same_level = top_bit[:, None, :] == level_ids[None, :, None]
    below = (same_level & (block_ids[None, None, :] < block_ids[:, None, None])).astype(jnp.float32)
    above = (same_level & (block_ids[None, None, :] > block_ids[:, None, None])).astype(jnp.float32)
    carry = jnp.einsum("cke,enp->cknp", below, state, precision=lax.Precision.HIGHEST).astype(jnp.bfloat16)
    far_lam = lam_block[:, :, low_bits + 1:low_bits + 1 + ctx_bits]
    rising = (far_lam[:, :, :, None] * cs_block[:, :, None, :].astype(jnp.float32)).astype(jnp.bfloat16)
    grad_state = jnp.einsum("clkn,clp->cknp", rising.astype(jnp.float32), ds_block.astype(jnp.float32))
    back_state = jnp.einsum("cke,eknp->cnp", above, grad_state, precision=lax.Precision.HIGHEST).astype(jnp.bfloat16)
    positions = jnp.arange(tok_rows, dtype=jnp.int32)
    local_level = bit_count(positions[:, None] ^ positions[None, :], low_bits)
    causal = positions[None, :] <= positions[:, None]

    def one_block(bundle):
        x_blk, b_blk, c_blk, d_blk, lam_blk, carry_blk, rise_blk, back_blk = bundle
        weight = jnp.take_along_axis(lam_blk, local_level, axis=1)
        weight = jnp.where(causal, weight, 0.0)
        scores = jnp.dot(c_blk, b_blk.T, preferred_element_type=jnp.float32)
        mixing = (scores * weight).astype(jnp.bfloat16)
        flat_carry = carry_blk.reshape(ctx_bits * NSTATE, feat_width)
        flat_rise = rise_blk.reshape(tok_rows, ctx_bits * NSTATE)
        y_blk = jnp.dot(mixing, x_blk, preferred_element_type=jnp.float32) + jnp.dot(flat_rise, flat_carry, preferred_element_type=jnp.float32)
        dx_blk = jnp.dot(mixing.T, d_blk, preferred_element_type=jnp.float32) + jnp.dot(b_blk, back_blk, preferred_element_type=jnp.float32)
        per_group = jnp.einsum("lgp,mgp->glm", d_blk.reshape(tok_rows, groups_head, -1).astype(jnp.float32), x_blk.reshape(tok_rows, groups_head, -1).astype(jnp.float32))
        d_mix = (per_group * weight[None]).astype(jnp.bfloat16).astype(jnp.float32)
        grad_c = jnp.einsum("glm,mn->ln", d_mix, b_blk.astype(jnp.float32))
        grad_b = jnp.einsum("glm,ln->mn", d_mix, c_blk.astype(jnp.float32))
        far_terms = jnp.dot(d_blk, flat_carry.T, preferred_element_type=jnp.float32).reshape(tok_rows, ctx_bits, NSTATE)
        grad_c = grad_c + jnp.sum(far_terms * lam_blk[:, low_bits + 1:low_bits + 1 + ctx_bits, None], axis=1)
        grad_b = grad_b + jnp.dot(x_blk, back_blk.T, preferred_element_type=jnp.float32)
        return y_blk.astype(jnp.bfloat16), dx_blk.astype(jnp.bfloat16), grad_b, grad_c

    y_all, dx_all, gb_all, gc_all = lax.map(one_block, (xs_block, bs_block, cs_block, ds_block, lam_block, carry, rising, back_state))
    total_rows = num_blocks * tok_rows
    return (y_all.reshape(total_rows, feat_width), dx_all.reshape(total_rows, feat_width), gb_all.reshape(total_rows, NSTATE), gc_all.reshape(total_rows, NSTATE))
```

```python
import contextlib
import functools

import jax
import jax.numpy as jnp
from jax import lax
from jax.experimental import pallas as pl
from jax.experimental.pallas import tpu as pltpu
from jax.sharding import PartitionSpec as P

F32 = jnp.float32
BF16 = jnp.bfloat16
MESH = pl.DeviceIdType.MESH
TILE = 256
WIDTH = 256
CHUNKS = 16
GROUPS = ((0, 8), (8, 14), (14, 16))
FAR_AT = ((21.5, 22.9), (25.3, 26.6), (26.8, 28.0))
EARLY = 2
BEAT = 0.7
UP_SPLIT = range(1, 15)
DOWN_SPLIT = range(1, 11)
TOP_SPLIT = range(12, 16)
VMEM_BYTES = 67043328
SPARE = 16384


def scope(name):
    return contextlib.nullcontext()


def mm(a, b):
    return jnp.dot(a, b, preferred_element_type=F32)


def mm_tn(a, b):
    return lax.dot_general(a, b, (((0,), (0,)), ((), ())), preferred_element_type=F32)


def mm_nt(a, b):
    return lax.dot_general(a, b, (((1,), (1,)), ((), ())), preferred_element_type=F32)


def bit_count(values, bits):
    counted = jnp.zeros(values.shape, jnp.int32)
    for digit_no in range(bits):
        counted = counted + (values >= 1 << digit_no).astype(jnp.int32)
    return counted


def kernel(
    count,
    heads,
    x_hbm,
    b_hbm,
    c_hbm,
    d_hbm,
    table_hbm,
    index_hbm,
    y_ref,
    dx_ref,
    db_ref,
    dc_ref,
    x_ref,
    d_ref,
    b_ref,
    c_ref,
    table_ref,
    index_ref,
    wide_table,
    w_ref,
    wt_ref,
    bt_ref,
    ct_ref,
    mix,
    d_mix,
    y_acc,
    dx_acc,
    grads,
    rise,
    rise_t,
    carry,
    back,
    s_buf,
    g_buf,
    rx0,
    up,
    rc,
    rb,
    tot,
    xb,
    rxb,
    hr,
    small_sem,
    x_sem,
    d_sem,
    x0_s,
    x0_r,
    up_s,
    fw_s,
    rc_r,
    ga_s,
    pr_s,
    bk_s,
    rb_r,
    xb_s,
    xb_r,
    hd_s,
    hd_r,
):
    bits = count.bit_length() - 1
    top = bits - 1
    toks, feats = x_ref.shape
    nstate = b_ref.shape[1]
    rows_q = nstate // CHUNKS
    blocks = toks // TILE
    part = toks // heads
    tile_bits = TILE.bit_length() - 1
    low_bits = toks.bit_length() - 1
    me = lax.axis_index("ctx")
    head = lax.axis_index("head")
    par = me % 2
    col = me // 2
    levels = range(1, bits)
    columns = count // 2
    split = bits >= 3
    is_set = {k: (me // (1 << k)) % 2 == 1 for k in range(bits)}
    low_top = {k: col % (1 << k) == (1 << (k - 1)) - 1 for k in levels}
    up_top = {k: col % (1 << k) == (1 << k) - 1 for k in levels}
    relay = {k: is_set[k] & jnp.logical_not(up_top[k]) for k in levels}
    last = col == columns - 1
    inner = jnp.logical_not(last)
    beside = col == columns - 2
    mine = (par == 0, par == 1)
    partner = me + 1 - 2 * par

    def splits_up(k, q):
        return split and k < top and q in UP_SPLIT

    def splits_down(k, q):
        return split and q in (DOWN_SPLIT if k < top else TOP_SPLIT)

    def owned(splits, k, line):
        return sum(not splits(k, q) or q % 2 == line for q in range(CHUNKS))

    def shared(splits, k, line):
        return sum(splits(k, q) and q % 2 == line for q in range(CHUNKS))

    def carried_up(k, q):
        return jnp.logical_not(beside) | mine[q % 2] if splits_up(k, q) else None

    def carried_down(k, q):
        return jnp.logical_not(beside) | mine[q % 2] if splits_down(k, q) else None

    def when(condition, body):
        if condition is None:
            body()
        else:
            pl.when(condition)(body)

    strips = feats // WIDTH
    loads = [
        pltpu.make_async_copy(hbm, vmem, small_sem.at[n])
        for n, (hbm, vmem) in enumerate(
            (
                (table_hbm, table_ref),
                (index_hbm, index_ref),
                (c_hbm, c_ref),
                (b_hbm, b_ref),
            )
        )
    ]
    halves = 2
    wide = feats // halves

    def fill_x(n):
        cols = pl.ds(n * wide, wide)
        return pltpu.make_async_copy(x_hbm.at[:, cols], x_ref.at[:, cols], x_sem.at[n])

    fill_d = pltpu.make_async_copy(d_hbm, d_ref, d_sem.at[0])
    for load in loads:
        load.start()
    for n in range(halves):
        fill_x(n).start()

    barrier = pltpu.get_barrier_semaphore()
    pl.semaphore_signal(barrier, inc=1, device_id={"ctx": partner}, device_id_type=MESH)

    @pl.when(col > 0)
    def _():
        pl.semaphore_signal(barrier, inc=1, device_id={"ctx": me - 2}, device_id_type=MESH)

    @pl.when(inner)
    def _():
        pl.semaphore_signal(barrier, inc=1, device_id={"ctx": me + 2}, device_id_type=MESH)

    peers = [(head + m) % heads for m in range(1, heads)]
    for peer in peers:
        pl.semaphore_signal(barrier, inc=1, device_id={"head": peer}, device_id_type=MESH)

    def remote(src, dst, ssem, rsem, device):
        return pltpu.make_async_remote_copy(
            src_ref=src,
            dst_ref=dst,
            send_sem=ssem,
            recv_sem=rsem,
            device_id=device,
            device_id_type=MESH,
        )

    def x0_copy(q):
        return remote(s_buf.at[q], rx0.at[q], x0_s.at[0], x0_r.at[q], {"ctx": partner})

    def up_copy(k, q):
        return remote(up.at[q], rc.at[k - 1, q], up_s.at[0], rc_r.at[k - 1, q], {"ctx": me + 2})

    def forward_copy(k, q):
        held = rc.at[k - 1, q]
        return remote(held, held, fw_s.at[k - 1], rc_r.at[k - 1, q], {"ctx": me + 2})

    def gather_copy(k, q):
        held = rc.at[k - 1, q]
        return remote(held, held, ga_s.at[k - 1], rc_r.at[k - 1, q], {"ctx": partner})

    def pre_copy(k, q):
        return remote(
            g_buf.at[k, q], rb.at[k - 1, q], pr_s.at[k - 1], rb_r.at[k - 1, q], {"ctx": partner}
        )

    def back_copy(k, q):
        return remote(
            g_buf.at[k, q], rb.at[k - 1, q], bk_s.at[k - 1], rb_r.at[k - 1, q], {"ctx": me - 2}
        )

    def group_of(q):
        return next(g for g, (q0, q1) in enumerate(GROUPS) if q0 <= q < q1)

    def xb_copy(q):
        return remote(xb.at[q], rxb.at[q], xb_s.at[0], xb_r.at[group_of(q)], {"ctx": partner})

    def xg_copy(q):
        return remote(
            g_buf.at[0, q], rxb.at[q], xb_s.at[0], xb_r.at[group_of(q)], {"ctx": partner}
        )

    def xb_all(q0, n, g):
        held = pl.ds(q0, n)
        return remote(xb.at[held], rxb.at[held], xb_s.at[0], xb_r.at[g], {"ctx": partner})

    with scope("tw"):
        loads[0].wait()
        loads[1].wait()
    with scope("w"):
        wide_table[...] = jnp.zeros_like(wide_table)
        wide_table[:, : table_ref.shape[1]] = table_ref[...]
        hot = (
            lax.broadcasted_iota(jnp.int32, (table_ref.shape[0], toks), 0) == index_ref[...]
        ).astype(F32)
        w_t = lax.dot_general(
            wide_table[...],
            hot,
            (((0,), (0,)), ((), ())),
            preferred_element_type=F32,
            precision=lax.Precision.HIGHEST,
        )
        wt_ref[...] = w_t
    with scope("cw"):
        loads[2].wait()
        loads[3].wait()
    fill_d.start()
    with scope("bc"):
        b_t = b_ref[...].astype(F32).T.astype(BF16)
        bt_ref[...] = b_t
        c_t = c_ref[...].astype(F32).T
        ct_ref[...] = c_t.astype(BF16)
        for k in range(bits):
            lam_t = w_t[low_bits + 1 + k : low_bits + 2 + k, :]
            rise_t[k * nstate : (k + 1) * nstate, :] = (c_t * lam_t).astype(BF16)
    for n in range(halves):
        with scope(f"xw{n}"):
            fill_x(n).wait()
        with scope(f"s{n}"):
            for q in range(n * wide // WIDTH, (n + 1) * wide // WIDTH):
                cols = slice(q * WIDTH, (q + 1) * WIDTH)
                s_buf[:, :, cols] = mm(b_t, x_ref[:, cols]).reshape(CHUNKS, rows_q, WIDTH)
    with scope("barrier"):
        ends = (col > 0).astype(jnp.int32) + inner.astype(jnp.int32)
        pl.semaphore_wait(barrier, heads + ends)

    for q in range(CHUNKS):
        wanted = inner
        if splits_up(1, q) and q % 2:
            wanted = inner & jnp.logical_not(beside & mine[1])
        pl.when(wanted | (last & mine[0]) if q < EARLY else wanted)(x0_copy(q).start)

    with scope("dw"):
        fill_d.wait()
    with scope("g"):
        for k in reversed(range(bits)):

            @pl.when(is_set[k])
            def _():
                for q in range(strips):
                    cols = slice(q * WIDTH, (q + 1) * WIDTH)
                    part_g = mm(rise_t[k * nstate : (k + 1) * nstate, :], d_ref[:, cols])
                    g_buf[k, :, :, cols] = part_g.reshape(CHUNKS, rows_q, WIDTH)

            if k:

                @pl.when(last)
                def _():
                    for q in range(CHUNKS):
                        if splits_down(k, q):
                            pl.when(mine[1 - q % 2])(pre_copy(k, q).start)
                        elif k == top:
                            back_copy(k, q).start()

            else:
                for q in range(EARLY):
                    pl.when(last & mine[1])(xg_copy(q).start)

                @pl.when(beside & mine[1])
                def _():
                    for q in range(CHUNKS):
                        if splits_down(1, q) and q % 2 == 0:
                            xg_copy(q).start()

    with scope("w2"):
        w_ref[...] = wt_ref[...].T
        carry[...] = jnp.zeros_like(carry)

        @pl.when(last)
        def _():
            tot[...] = jnp.zeros_like(tot)

        pl.when(last & mine[1])(lambda: rxb.__setitem__(..., jnp.zeros_like(rxb)))
        if split:

            @pl.when(beside & mine[1])
            def _():
                for q in range(CHUNKS):
                    if splits_down(1, q) and q % 2:
                        rxb[q] = jnp.zeros_like(rxb[q])

    half = TILE // 2

    def diagonal(w_rows):
        row = lax.broadcasted_iota(jnp.int32, (half, half), 0)
        at = lax.broadcasted_iota(jnp.int32, (half, half), 1)
        differ = row ^ at
        weight = jnp.broadcast_to(w_rows[:, 0:1], (half, half))
        for n in range(tile_bits - 1):
            weight = jnp.where(differ >= 1 << n, w_rows[:, n + 1 : n + 2], weight)
        return jnp.where(at <= row, weight, 0.0)

    def weigh(i):
        rows = slice(i * TILE, (i + 1) * TILE)
        w_rows = w_ref[rows, :]
        upper, lower = w_rows[:half], w_rows[half:]
        side = jnp.broadcast_to(lower[:, tile_bits : tile_bits + 1], (half, half))
        weight = jnp.concatenate(
            [
                jnp.concatenate([diagonal(upper), jnp.zeros((half, half), F32)], axis=1),
                jnp.concatenate([side, diagonal(lower)], axis=1),
            ],
            axis=0,
        )
        c_i, d_i = c_ref[rows, :], d_ref[rows, :]
        for j in range(i + 1):
            cols = slice(j * TILE, (j + 1) * TILE)
            if j < i:
                level = tile_bits + (i ^ j).bit_length()
                factor = w_rows[:, level : level + 1]
            else:
                factor = weight
            mix[rows, cols] = (mm_nt(c_i, b_ref[cols, :]) * factor).astype(BF16)
            d_mix[rows, cols] = (mm_nt(d_i, x_ref[cols, :]) * factor).astype(BF16)

    def near_y(i):
        rows = slice(i * TILE, (i + 1) * TILE)
        seen = slice(0, (i + 1) * TILE)
        y_acc[rows, :] = mm(mix[rows, seen], x_ref[seen, :])
        grads[1, :, rows] = mm_nt(bt_ref[:, seen], d_mix[rows, seen])

    def near_dx(j):
        cols = slice(j * TILE, (j + 1) * TILE)
        seen = slice(j * TILE, toks)
        dx_acc[cols, :] = mm_tn(mix[seen, cols], d_ref[seen, :])
        grads[0, :, cols] = mm(ct_ref[:, seen], d_mix[seen, cols])

    def source(k, q):
        here = low_top[k]
        if k == 1 and splits_up(1, q):
            here = here & jnp.logical_not(beside & mine[1 - q % 2])
            if q % 2 == 0:
                pl.when(beside & mine[1])(x0_copy(q).wait_recv)

        @pl.when(here)
        def _():
            x0_copy(q).wait_recv()
            group = s_buf[q] + rx0[q]
            for j in range(1, k):
                up_copy(j, q).wait_recv()
                group = group + rc[j - 1, q]
            up[q] = group
            up_copy(k, q).start()

    def relay_up(k, q):
        @pl.when(relay[k])
        def _():
            up_copy(k, q).wait_recv()
            when(carried_up(k, q), forward_copy(k, q).start)

    def gather(k, q):
        @pl.when(last & mine[q % 2])
        def _():
            up_copy(k, q).wait_recv()
            gather_copy(k, q).start()

    def descend(k, q):
        if splits_down(k, q):

            @pl.when(last & mine[q % 2])
            def _():
                pre_copy(k, q).wait_recv()
                g_buf[k, q] = g_buf[k, q] + rb[k - 1, q]
                back_copy(k, q).start()

        else:
            pl.when(last)(back_copy(k, q).start)

    def relay_down(k, q):
        @pl.when(relay[k])
        def _():
            def add():
                back_copy(k, q).wait_recv()
                g_buf[k, q] = g_buf[k, q] + rb[k - 1, q]

            when(carried_down(k, q), add)
            back_copy(k, q).start()

    def cross(q):
        @pl.when(mine[1])
        def _():
            xb[q] = tot[q] + g_buf[0, q]

        @pl.when(mine[0])
        def _():
            xb[q] = tot[q]

    def pass_down(k, q):
        here = low_top[k] & jnp.logical_not(beside) if split else low_top[k]

        @pl.when(here)
        def _():
            back_copy(k, q).wait_recv()
            got = rb[k - 1, q]
            tot[q] = got
            for j in range(1, k):
                g_buf[j, q] = g_buf[j, q] + got
                back_copy(j, q).start()
            cross(q)
            xb_copy(q).start()

    def beside_down(q):
        def own():
            back_copy(1, q).wait_recv()
            tot[q] = rb[0, q]
            cross(q)
            xb_copy(q).start()

        if splits_down(1, q):
            pl.when(beside & mine[q % 2])(own)

            @pl.when(beside & mine[1 - q % 2])
            def _():
                tot[q] = jnp.zeros_like(tot[q])

        else:
            pl.when(beside)(own)

    def spread(array, g):
        n0, n1 = GROUPS[g][0] * rows_q, GROUPS[g][1] * rows_q
        copies = []
        for m, peer in enumerate(peers):
            lanes = pl.ds(pl.multiple_of(peer * part, part), part)
            copies.append(
                remote(
                    grads.at[array, pl.ds(n0, n1 - n0), lanes],
                    hr.at[m, array, pl.ds(n0, n1 - n0)],
                    hd_s.at[0],
                    hd_r.at[array, g],
                    {"head": peer},
                )
            )
        return copies

    def far_up(g):
        q0, q1 = GROUPS[g]
        n0, n1 = q0 * rows_q, q1 * rows_q
        for q in range(q0, q1):
            pl.when(last & mine[1])(x0_copy(q).wait_recv)
            for k in levels:
                if splits_up(k, q):
                    pl.when(last & mine[1 - q % 2])(gather_copy(k, q).wait_recv)
                else:
                    pl.when(last)(up_copy(k, q).wait_recv)
        for k in range(bits):

            @pl.when(is_set[k])
            def _():
                got = rc[k - 1, q0:q1] if k else rx0[q0:q1]
                carry[k * nstate + n0 : k * nstate + n1, :] = got.reshape(n1 - n0, feats).astype(BF16)

        held = [carry[k * nstate + n0 : k * nstate + n1, :] for k in range(bits)]
        terms = mm_nt(jnp.concatenate(held, axis=0), d_ref[...])
        total = grads[1, n0:n1, :]
        for k in range(bits):
            lam = wt_ref[low_bits + 1 + k : low_bits + 2 + k, :]
            total = total + terms[k * (n1 - n0) : (k + 1) * (n1 - n0), :] * lam
        grads[1, n0:n1, :] = total
        for copy in spread(1, g):
            copy.start()

    def far_down(g):
        q0, q1 = GROUPS[g]
        n0, n1 = q0 * rows_q, q1 * rows_q
        pl.when(mine[0] | jnp.logical_not(last | beside) if split else mine[0] | inner)(
            xb_all(q0, q1 - q0, g).wait_recv
        )
        if split:
            given = sum(not splits_down(1, q) or q % 2 == 0 for q in range(q0, q1))
            pl.when(beside & mine[1])(xb_all(q0, given, g).wait_recv)
        held = (tot[q0:q1] + rxb[q0:q1]).reshape(n1 - n0, feats).astype(BF16)
        back[n0:n1, :] = held
        grads[0, n0:n1, :] = grads[0, n0:n1, :] + mm_nt(held, x_ref[...])
        for copy in spread(0, g):
            copy.start()

    def late_sends(q):
        pl.when(last & mine[0])(x0_copy(q).start)
        pl.when(last & mine[1])(xg_copy(q).start)

    def rises():
        c_f = c_ref[...].astype(F32)
        for k in range(bits):
            lam = w_ref[:, low_bits + 1 + k : low_bits + 2 + k]
            rise[:, k * nstate : (k + 1) * nstate] = (c_f * lam).astype(BF16)

    plan = []

    def put(time, name, step, *args):
        plan.append((time, len(plan), name, step, args))

    def rise_at(k, q):
        return (6.4 if k == 1 else 9.1 + 5.8 * (k - 2)) + BEAT * q

    def fall_at(k, q):
        return 10.6 + 3.4 * (top - k) + BEAT * q

    for q in range(CHUNKS):
        for k in levels:
            put(rise_at(k, q), "source", source, k, q)
            put(fall_at(k, q), "pass_down", pass_down, k, q)
            if k > 1:
                put(rise_at(k, q) + 2.9, "relay_up", relay_up, k, q)
                put(7.1 + BEAT * q if k == top else fall_at(k, q) - 1.4, "relay_down", relay_down, k, q)
            if splits_up(k, q):
                put(rise_at(k, q) + 3.1, "gather", gather, k, q)
            if k < top:
                put(9.4 + 0.28 * q, "descend", descend, k, q)
            elif splits_down(k, q):
                put(8.4 + 0.2 * (q - TOP_SPLIT[0]), "descend", descend, k, q)
        if split:
            put(17.0 + 0.45 * q, "beside", beside_down, q)
        if q >= EARLY:
            put(8.0 + 0.95 * (q - EARLY), "late", late_sends, q)
    deeper = max(top - 2, 0)
    for g, (up_at, down_at) in enumerate(FAR_AT):
        put(up_at + 5.8 * deeper, "far_up", far_up, g)
        put(down_at + 3.4 * deeper, "far_down", far_down, g)
    near = [(weigh, 0)]
    for i in range(1, blocks):
        near += [(weigh, i), (near_y, i - 1)]
    near += [(near_y, blocks - 1)] + [(near_dx, j) for j in range(blocks)]
    for n, (step, i) in enumerate(near):
        put(4.6 + 13.5 / len(near) * n, step.__name__, step, i)
    put(20.0, "rises", rises)
    for _, _, name, step, args in sorted(plan, key=lambda item: item[:2]):
        with scope(name + "_" + "_".join(str(a) for a in args)):
            step(*args)

    with scope("y"):
        for q in range(strips):
            cols = slice(q * WIDTH, (q + 1) * WIDTH)
            y_ref[:, cols] = (y_acc[:, cols] + mm(rise[...], carry[:, cols])).astype(BF16)
    with scope("dx"):
        for q in range(strips):
            cols = slice(q * WIDTH, (q + 1) * WIDTH)
            dx_ref[:, cols] = (dx_acc[:, cols] + mm(b_ref[...], back[:, cols])).astype(BF16)
    own = pl.ds(pl.multiple_of(head * part, part), part)
    for g, (q0, q1) in enumerate(GROUPS):
        rows = pl.ds(q0 * rows_q, (q1 - q0) * rows_q)
        for array in (1, 0):
            with scope(f"heads_{g}_{array}"):
                total = grads[array, rows, own]
                if heads > 1:
                    given = hr.at[:, array, rows]
                    remote(given, given, hd_s.at[0], hd_r.at[array, g], {"head": peers[0]}).wait_recv()
                    for m in range(heads - 1):
                        total = total + hr[m, array, rows]
                (db_ref, dc_ref)[array][:, rows] = total.T

    def sent(sem, n, condition):
        if n:
            held = s_buf.at[pl.ds(0, n)]
            pl.when(condition)(remote(held, held, sem, x0_r.at[0], {"ctx": partner}).wait_send)

    with scope("drain"):
        if heads > 1:
            remote(hr, hr, hd_s.at[0], hd_r.at[0, 0], {"head": peers[0]}).wait_send()
        if split:
            apart = jnp.logical_not(beside)
            sent(x0_s.at[0], CHUNKS, (inner & apart) | mine[0])
            sent(x0_s.at[0], owned(splits_up, 1, 0), beside & mine[1])
            sent(xb_s.at[0], CHUNKS, (inner & apart) | mine[1])
            sent(xb_s.at[0], owned(splits_down, 1, 0), beside & mine[0])
        else:
            sent(x0_s.at[0], CHUNKS, inner | mine[0])
            sent(xb_s.at[0], CHUNKS, inner | mine[1])
        for k in levels:
            for line in range(2):
                full = mine[line] & jnp.logical_not(beside)
                edge = mine[line] & beside
                sent(up_s.at[0], CHUNKS, low_top[k] & full)
                sent(up_s.at[0], owned(splits_up, k, line), low_top[k] & edge)
                sent(fw_s.at[k - 1], CHUNKS, relay[k] & full)
                sent(fw_s.at[k - 1], owned(splits_up, k, line), relay[k] & edge)
                sent(ga_s.at[k - 1], shared(splits_up, k, line), last & mine[line])
                sent(pr_s.at[k - 1], shared(splits_down, k, 1 - line), last & mine[line])
                sent(bk_s.at[k - 1], CHUNKS, is_set[k] & mine[line] & inner)
                sent(bk_s.at[k - 1], owned(splits_down, k, line), last & mine[line])


def write_out(*refs):
    copies = [pltpu.make_async_copy(refs[n], refs[n + 4], refs[8].at[n]) for n in range(4)]
    for copy in copies:
        copy.start()
    for copy in copies:
        copy.wait()


def local(x_in, b_in, c_in, d_out, table, level_index):
    toks, feats = x_in.shape
    nstate = b_in.shape[1]
    count, heads = lax.axis_size("ctx"), lax.axis_size("head")
    bits = count.bit_length() - 1
    strips = feats // WIDTH
    index = level_index.reshape(1, toks)
    rows = toks // heads
    ups = max(bits - 1, 1)
    others = max(heads - 1, 1)
    vmem = pl.BlockSpec(memory_space=pltpu.VMEM)
    hbm = pl.BlockSpec(memory_space=pltpu.HBM)
    dma = pltpu.SemaphoreType.DMA
    slab = (CHUNKS, nstate // CHUNKS, feats)
    results = pl.pallas_call(
        functools.partial(kernel, count, heads),
        out_shape=(
            pltpu.VMEM((toks, feats), BF16),
            pltpu.VMEM((toks, feats), BF16),
            pltpu.VMEM((rows, nstate), F32),
            pltpu.VMEM((rows, nstate), F32),
        ),
        in_specs=[hbm] * 6,
        out_specs=(vmem,) * 4,
        scratch_shapes=[
            pltpu.VMEM((toks, feats), BF16),
            pltpu.VMEM((toks, feats), BF16),
            pltpu.VMEM((toks, nstate), BF16),
            pltpu.VMEM((toks, nstate), BF16),
            pltpu.VMEM(table.shape, F32),
            pltpu.VMEM((1, toks), jnp.int32),
            pltpu.VMEM((table.shape[0], nstate), F32),
            pltpu.VMEM((toks, nstate), F32),
            pltpu.VMEM((nstate, toks), F32),
            pltpu.VMEM((nstate, toks), BF16),
            pltpu.VMEM((nstate, toks), BF16),
            pltpu.VMEM((toks, toks), BF16),
            pltpu.VMEM((toks, toks), BF16),
            pltpu.VMEM((toks, feats), F32),
            pltpu.VMEM((toks, feats), F32),
            pltpu.VMEM((2, nstate, toks), F32),
            pltpu.VMEM((toks, bits * nstate), BF16),
            pltpu.VMEM((bits * nstate, toks), BF16),
            pltpu.VMEM((bits * nstate, feats), BF16),
            pltpu.VMEM((nstate, feats), BF16),
            pltpu.VMEM(slab, F32),
            pltpu.VMEM((bits,) + slab, F32),
            pltpu.VMEM(slab, F32),
            pltpu.VMEM(slab, F32),
            pltpu.VMEM((ups,) + slab, F32),
            pltpu.VMEM((ups,) + slab, F32),
            pltpu.VMEM(slab, F32),
            pltpu.VMEM(slab, F32),
            pltpu.VMEM(slab, F32),
            pltpu.VMEM((others, 2, nstate, rows), F32),
            dma((4,)),
            dma((2,)),
            dma((1,)),
            dma((1,)),
            dma((CHUNKS,)),
            dma((1,)),
            dma((ups,)),
            dma((ups, CHUNKS)),
            dma((ups,)),
            dma((ups,)),
            dma((ups,)),
            dma((ups, CHUNKS)),
            dma((1,)),
            dma((len(GROUPS),)),
            dma((1,)),
            dma((2, len(GROUPS))),
        ],
        compiler_params=pltpu.CompilerParams(
            collective_id=0,
            has_side_effects=True,
            vmem_limit_bytes=VMEM_BYTES - 4 * toks * feats - 8 * rows * nstate - SPARE,
        ),
    )(x_in, b_in, c_in, d_out, table, index)
    return pl.pallas_call(
        write_out,
        out_shape=tuple(jax.ShapeDtypeStruct(r.shape, r.dtype) for r in results),
        in_specs=[vmem] * 4,
        out_specs=(hbm,) * 4,
        scratch_shapes=[dma((4,))],
        compiler_params=pltpu.CompilerParams(vmem_limit_bytes=1024 * 1024),
    )(*results)


def solution(mesh):
    return jax.shard_map(
        local,
        mesh=mesh,
        in_specs=(
            P("ctx", "head"),
            P("ctx", None),
            P("ctx", None),
            P("ctx", "head"),
            P(),
            P("ctx"),
        ),
        out_specs=(
            P("ctx", "head"),
            P("ctx", "head"),
            P(("ctx", "head"), None),
            P(("ctx", "head"), None),
        ),
        check_vma=False,
    )
```

```python
import contextlib
import functools

import jax
import jax.numpy as jnp
from jax import lax
from jax.experimental import pallas as pl
from jax.experimental.pallas import tpu as pltpu
from jax.sharding import PartitionSpec as P

F32 = jnp.float32
BF16 = jnp.bfloat16
MESH = pl.DeviceIdType.MESH
TILE = 256
WIDTH = 256
CHUNKS = 16
GROUPS = ((0, 8), (8, 14), (14, 16))
FIRST_AT = ((13.5, 16.6, 18.4), (22.6, 26.5, 28.0), (16.9, 19.9), (25.2, 27.6), (19.3, 20.7))
INNER_AT = ((18.9, 22.3, 23.5), (24.0, 26.5, 28.0), (21.9, 25.2), (26.3, 27.6), (24.4, 25.5))
LAST_AT = ((24.0, 27.2, 28.8), (23.0, 25.8, 27.9), (25.9, 28.7), (25.5, 28.4), (29.6, 30.2))
EARLY = 2
BEAT = 0.7
UP_SPLIT = range(4, 16)
DOWN_SPLIT = range(1, 11)
TOP_SPLIT = range(12, 16)
VMEM_BYTES = 67043328
SPARE = 16384


def scope(name):
    return contextlib.nullcontext()


def mm(a, b):
    return jnp.dot(a, b, preferred_element_type=F32)


def mm_tn(a, b):
    return lax.dot_general(a, b, (((0,), (0,)), ((), ())), preferred_element_type=F32)


def mm_nt(a, b):
    return lax.dot_general(a, b, (((1,), (1,)), ((), ())), preferred_element_type=F32)


def bit_count(values, bits):
    counted = jnp.zeros(values.shape, jnp.int32)
    for digit_no in range(bits):
        counted = counted + (values >= 1 << digit_no).astype(jnp.int32)
    return counted


def kernel(
    count,
    heads,
    x_hbm,
    b_hbm,
    c_hbm,
    d_hbm,
    table_hbm,
    index_hbm,
    y_ref,
    dx_ref,
    db_ref,
    dc_ref,
    x_ref,
    d_ref,
    b_ref,
    c_ref,
    table_ref,
    index_ref,
    wide_table,
    w_ref,
    wt_ref,
    bt_ref,
    ct_ref,
    mix,
    d_mix,
    y_acc,
    dx_acc,
    grads,
    rise,
    rise_t,
    carry,
    back,
    s_buf,
    g_buf,
    rx0,
    up,
    rc,
    rb,
    tot,
    xb,
    rxb,
    hr,
    h1,
    sums,
    small_sem,
    x_sem,
    d_sem,
    x0_s,
    x0_r,
    up_s,
    fw_s,
    rc_r,
    ga_s,
    pr_s,
    bk_s,
    rb_r,
    xb_s,
    xb_r,
    hd_s,
    hd_r,
    h1_r,
):
    bits = count.bit_length() - 1
    top = bits - 1
    toks, feats = x_ref.shape
    nstate = b_ref.shape[1]
    rows_q = nstate // CHUNKS
    blocks = toks // TILE
    part = toks // heads
    tile_bits = TILE.bit_length() - 1
    low_bits = toks.bit_length() - 1
    me = lax.axis_index("ctx")
    head = lax.axis_index("head")
    par = me % 2
    col = me // 2
    levels = range(1, bits)
    columns = count // 2
    split = bits >= 3
    is_set = {k: (me // (1 << k)) % 2 == 1 for k in range(bits)}
    low_top = {k: col % (1 << k) == (1 << (k - 1)) - 1 for k in levels}
    up_top = {k: col % (1 << k) == (1 << k) - 1 for k in levels}
    relay = {k: is_set[k] & jnp.logical_not(up_top[k]) for k in levels}
    last = col == columns - 1
    inner = jnp.logical_not(last)
    beside = col == columns - 2
    mine = (par == 0, par == 1)
    partner = me + 1 - 2 * par

    def splits_up(k, q):
        return split and k < top and q in UP_SPLIT

    def splits_down(k, q):
        return split and q in (DOWN_SPLIT if k < top else TOP_SPLIT)

    def owned(splits, k, line):
        return sum(not splits(k, q) or q % 2 == line for q in range(CHUNKS))

    def shared(splits, k, line):
        return sum(splits(k, q) and q % 2 == line for q in range(CHUNKS))

    first = col == 0
    classes = (first & inner, inner & jnp.logical_not(first), last)

    def carried_up(k, q):
        return jnp.logical_not(beside) | mine[q % 2] if splits_up(k, q) else None

    def carried_down(k, q):
        return jnp.logical_not(beside) | mine[q % 2] if splits_down(k, q) else None

    def when(condition, body):
        if condition is None:
            body()
        else:
            pl.when(condition)(body)

    strips = feats // WIDTH
    loads = [
        pltpu.make_async_copy(hbm, vmem, small_sem.at[n])
        for n, (hbm, vmem) in enumerate(
            (
                (table_hbm, table_ref),
                (index_hbm, index_ref),
                (c_hbm, c_ref),
                (b_hbm, b_ref),
            )
        )
    ]
    halves = 4
    wide = feats // halves

    def fill_x(n):
        cols = pl.ds(n * wide, wide)
        return pltpu.make_async_copy(x_hbm.at[:, cols], x_ref.at[:, cols], x_sem.at[n])

    fill_d = pltpu.make_async_copy(d_hbm, d_ref, d_sem.at[0])
    def load_states():
        loads[3].start()
        for n in range(halves):
            fill_x(n).start()

    def load_weights():
        for load in loads[:3]:
            load.start()

    @pl.when(inner)
    def _():
        load_states()
        load_weights()

    @pl.when(last)
    def _():
        load_weights()
        fill_d.start()

    barrier = pltpu.get_barrier_semaphore()
    pl.semaphore_signal(barrier, inc=1, device_id={"ctx": partner}, device_id_type=MESH)

    @pl.when(col > 0)
    def _():
        pl.semaphore_signal(barrier, inc=1, device_id={"ctx": me - 2}, device_id_type=MESH)

    @pl.when(inner)
    def _():
        pl.semaphore_signal(barrier, inc=1, device_id={"ctx": me + 2}, device_id_type=MESH)

    peers = [(head + m) % heads for m in range(1, heads)]
    for peer in peers:
        pl.semaphore_signal(barrier, inc=1, device_id={"head": peer}, device_id_type=MESH)

    def remote(src, dst, ssem, rsem, device):
        return pltpu.make_async_remote_copy(
            src_ref=src,
            dst_ref=dst,
            send_sem=ssem,
            recv_sem=rsem,
            device_id=device,
            device_id_type=MESH,
        )

    def x0_copy(q):
        return remote(s_buf.at[q], rx0.at[q], x0_s.at[0], x0_r.at[q], {"ctx": partner})

    def fall_sem(k, q):
        return rb_r.at[k - 2, q] if k > 1 else rc_r.at[0, q]

    def up_copy(k, q):
        return remote(up.at[q], rc.at[k - 1, q], up_s.at[0], rc_r.at[k - 1, q], {"ctx": me + 2})

    def forward_copy(k, q):
        held = rc.at[k - 1, q]
        return remote(held, held, fw_s.at[k - 1], rc_r.at[k - 1, q], {"ctx": me + 2})

    def gather_copy(k, q):
        held = rc.at[k - 1, q]
        return remote(held, held, ga_s.at[k - 1], rc_r.at[k - 1, q], {"ctx": partner})

    def pre_copy(k, q):
        return remote(
            g_buf.at[k, q], rb.at[k - 1, q], pr_s.at[k - 1], fall_sem(k if k > 1 else top, q), {"ctx": partner}
        )

    def back_copy(k, q):
        return remote(
            g_buf.at[k, q], rb.at[k - 1, q], bk_s.at[k - 1], fall_sem(k, q), {"ctx": me - 2}
        )

    def group_of(q):
        return next(g for g, (q0, q1) in enumerate(GROUPS) if q0 <= q < q1)

    def xb_copy(q):
        return remote(xb.at[q], rxb.at[q], xb_s.at[0], xb_r.at[group_of(q)], {"ctx": partner})

    def xg_copy(q):
        return remote(
            g_buf.at[0, q], rxb.at[q], xb_s.at[0], xb_r.at[group_of(q)], {"ctx": partner}
        )

    def xb_all(q0, n, g):
        held = pl.ds(q0, n)
        return remote(xb.at[held], rxb.at[held], xb_s.at[0], xb_r.at[g], {"ctx": partner})

    def states():
        with scope("b"):
            b_t = b_ref[...].astype(F32).T.astype(BF16)
            bt_ref[...] = b_t
        with scope("xw"):
            for n in range(halves):
                fill_x(n).wait()
        with scope("s"):
            for n in range(halves):
                cols = slice(n * wide, (n + 1) * wide)
                s_buf[:, :, cols] = mm(b_t, x_ref[:, cols]).reshape(CHUNKS, rows_q, wide)

    def weights():
        wide_table[...] = jnp.zeros_like(wide_table)
        wide_table[:, : table_ref.shape[1]] = table_ref[...]
        hot = (
            lax.broadcasted_iota(jnp.int32, (table_ref.shape[0], toks), 0) == index_ref[...]
        ).astype(F32)
        w_t = lax.dot_general(
            wide_table[...],
            hot,
            (((0,), (0,)), ((), ())),
            preferred_element_type=F32,
            precision=lax.Precision.HIGHEST,
        )
        wt_ref[...] = w_t
        c_t = c_ref[...].astype(F32).T
        ct_ref[...] = c_t.astype(BF16)
        for k in range(bits):
            lam_t = w_t[low_bits + 1 + k : low_bits + 2 + k, :]
            rise_t[k * nstate : (k + 1) * nstate, :] = (c_t * lam_t).astype(BF16)

    def meet():
        ends = (col > 0).astype(jnp.int32) + inner.astype(jnp.int32)
        pl.semaphore_wait(barrier, heads + ends)

    @pl.when(inner)
    def _():
        with scope("bw"):
            loads[3].wait()
        fill_d.start()
        states()
        with scope("barrier"):
            meet()
        for q in range(CHUNKS):
            if splits_up(1, q) and q % 2:
                pl.when(jnp.logical_not(beside & mine[1]))(x0_copy(q).start)
            else:
                x0_copy(q).start()
        with scope("tw"):
            for load in loads[:3]:
                load.wait()
        with scope("w"):
            weights()

    @pl.when(last)
    def _():
        with scope("tw"):
            for load in loads[:3]:
                load.wait()
        load_states()
        with scope("w"):
            weights()

    with scope("dw"):
        fill_d.wait()
    for k in reversed(range(bits)):
        with scope(f"g{k}"):

            @pl.when(is_set[k])
            def _():
                for q in range(strips):
                    cols = slice(q * WIDTH, (q + 1) * WIDTH)
                    part_g = mm(rise_t[k * nstate : (k + 1) * nstate, :], d_ref[:, cols])
                    g_buf[k, :, :, cols] = part_g.reshape(CHUNKS, rows_q, WIDTH)

        @pl.when(last)
        def _():
            if k == top:
                meet()
            for q in range(CHUNKS if k else 0):
                if splits_down(k, q):
                    pl.when(mine[1 - q % 2])(pre_copy(k, q).start)
                elif k == top:
                    back_copy(k, q).start()
            if k == 0:
                for q in range(EARLY):
                    pl.when(mine[1])(xg_copy(q).start)

        if k == 0:

            @pl.when(beside & mine[1])
            def _():
                for q in range(CHUNKS):
                    if splits_down(1, q) and q % 2 == 0:
                        xg_copy(q).start()

    @pl.when(last)
    def _():
        loads[3].wait()
        states()
        for q in range(EARLY):
            pl.when(mine[0])(x0_copy(q).start)

    with scope("w2"):
        w_ref[...] = wt_ref[...].T
        carry[...] = jnp.zeros_like(carry)

        @pl.when(last)
        def _():
            tot[...] = jnp.zeros_like(tot)

        pl.when(last & mine[1])(lambda: rxb.__setitem__(..., jnp.zeros_like(rxb)))
        if split:

            @pl.when(beside & mine[1])
            def _():
                for q in range(CHUNKS):
                    if splits_down(1, q) and q % 2:
                        rxb[q] = jnp.zeros_like(rxb[q])

    half = TILE // 2

    def diagonal(w_rows):
        row = lax.broadcasted_iota(jnp.int32, (half, half), 0)
        at = lax.broadcasted_iota(jnp.int32, (half, half), 1)
        differ = row ^ at
        weight = jnp.broadcast_to(w_rows[:, 0:1], (half, half))
        for n in range(tile_bits - 1):
            weight = jnp.where(differ >= 1 << n, w_rows[:, n + 1 : n + 2], weight)
        return jnp.where(at <= row, weight, 0.0)

    def weigh(i):
        rows = slice(i * TILE, (i + 1) * TILE)
        w_rows = w_ref[rows, :]
        upper, lower = w_rows[:half], w_rows[half:]
        side = jnp.broadcast_to(lower[:, tile_bits : tile_bits + 1], (half, half))
        weight = jnp.concatenate(
            [
                jnp.concatenate([diagonal(upper), jnp.zeros((half, half), F32)], axis=1),
                jnp.concatenate([side, diagonal(lower)], axis=1),
            ],
            axis=0,
        )
        c_i, d_i = c_ref[rows, :], d_ref[rows, :]
        for j in range(i + 1):
            cols = slice(j * TILE, (j + 1) * TILE)
            if j < i:
                level = tile_bits + (i ^ j).bit_length()
                factor = w_rows[:, level : level + 1]
            else:
                factor = weight
            mix[rows, cols] = (mm_nt(c_i, b_ref[cols, :]) * factor).astype(BF16)
            d_mix[rows, cols] = (mm_nt(d_i, x_ref[cols, :]) * factor).astype(BF16)

    def near_y(i):
        rows = slice(i * TILE, (i + 1) * TILE)
        seen = slice(0, (i + 1) * TILE)
        y_acc[rows, :] = mm(mix[rows, seen], x_ref[seen, :])
        grads[1, :, rows] = mm_nt(bt_ref[:, seen], d_mix[rows, seen])

    def near_dx(j):
        cols = slice(j * TILE, (j + 1) * TILE)
        seen = slice(j * TILE, toks)
        dx_acc[cols, :] = mm_tn(mix[seen, cols], d_ref[seen, :])
        grads[0, :, cols] = mm(ct_ref[:, seen], d_mix[seen, cols])

    def source(k, q):
        here = low_top[k]
        if k == 1 and splits_up(1, q):
            here = here & jnp.logical_not(beside & mine[1 - q % 2])
            if q % 2 == 0:
                pl.when(beside & mine[1])(x0_copy(q).wait_recv)

        @pl.when(here)
        def _():
            x0_copy(q).wait_recv()
            group = s_buf[q] + rx0[q]
            for j in range(1, k):
                up_copy(j, q).wait_recv()
                group = group + rc[j - 1, q]
            up[q] = group
            up_copy(k, q).start()

    def relay_up(k, q):
        @pl.when(relay[k])
        def _():
            up_copy(k, q).wait_recv()
            when(carried_up(k, q), forward_copy(k, q).start)

    def gather(k, q):
        @pl.when(last & mine[q % 2])
        def _():
            up_copy(k, q).wait_recv()
            gather_copy(k, q).start()

    def descend(k, q):
        if splits_down(k, q):

            @pl.when(last & mine[q % 2])
            def _():
                pre_copy(k, q).wait_recv()
                g_buf[k, q] = g_buf[k, q] + rb[k - 1, q]
                back_copy(k, q).start()

        else:
            pl.when(last)(back_copy(k, q).start)

    def relay_down(k, q):
        @pl.when(relay[k])
        def _():
            def add():
                back_copy(k, q).wait_recv()
                g_buf[k, q] = g_buf[k, q] + rb[k - 1, q]

            when(carried_down(k, q), add)
            back_copy(k, q).start()

    def cross(q):
        @pl.when(mine[1])
        def _():
            xb[q] = tot[q] + g_buf[0, q]

        @pl.when(mine[0])
        def _():
            xb[q] = tot[q]

    def pass_down(k, q):
        here = low_top[k] & jnp.logical_not(beside) if split else low_top[k]

        @pl.when(here)
        def _():
            back_copy(k, q).wait_recv()
            got = rb[k - 1, q]
            tot[q] = got
            for j in range(1, k):
                g_buf[j, q] = g_buf[j, q] + got
                back_copy(j, q).start()
            cross(q)
            xb_copy(q).start()

    def beside_down(q):
        def own():
            back_copy(1, q).wait_recv()
            tot[q] = rb[0, q]
            cross(q)
            xb_copy(q).start()

        if splits_down(1, q):
            pl.when(beside & mine[q % 2])(own)

            @pl.when(beside & mine[1 - q % 2])
            def _():
                tot[q] = jnp.zeros_like(tot[q])

        else:
            pl.when(beside)(own)

    final = len(GROUPS) - 1
    pair = head % 2
    fellow = head + 1 - 2 * pair
    ways = heads // 2

    def lanes_of(h):
        return pl.ds(pl.multiple_of(h * part, part), part)

    def rows_of(g):
        return pl.ds(GROUPS[g][0] * rows_q, (GROUPS[g][1] - GROUPS[g][0]) * rows_q)

    def spread(array, g):
        rows = rows_of(g)
        if g == final:
            for m, peer in enumerate(peers):
                remote(
                    grads.at[array, rows, lanes_of(peer)],
                    hr.at[m, array, rows],
                    hd_s.at[0],
                    hd_r.at[array, g],
                    {"head": peer},
                ).start()
        else:
            for j in range(ways):
                remote(
                    grads.at[array, rows, lanes_of(2 * j + 1 - pair)],
                    h1.at[j, array, rows],
                    hd_s.at[1],
                    h1_r.at[array, g],
                    {"head": fellow},
                ).start()

    def middle(array, g):
        rows = rows_of(g)
        if ways:
            given = h1.at[:, array, rows]
            remote(given, given, hd_s.at[1], h1_r.at[array, g], {"head": fellow}).wait_recv()
        for m in range(max(ways, 1)):
            j = (head // 2 + m) % max(ways, 1)
            total = grads[array, rows, lanes_of(2 * j + pair)]
            if ways:
                total = total + h1[j, array, rows]
            sums[m, array, rows] = total
            if m:
                remote(
                    sums.at[m, array, rows],
                    hr.at[m - 1, array, rows],
                    hd_s.at[2],
                    hd_r.at[array, g],
                    {"head": 2 * j + pair},
                ).start()

    def far_up(g, which):
        ending = which == 2
        q0, q1 = GROUPS[g]
        n0, n1 = q0 * rows_q, q1 * rows_q

        @pl.when(classes[which])
        def _():
            for q in range(q0, q1) if ending else ():
                pl.when(mine[1])(x0_copy(q).wait_recv)
                for k in levels:
                    if splits_up(k, q):
                        pl.when(mine[1 - q % 2])(gather_copy(k, q).wait_recv)
                    else:
                        up_copy(k, q).wait_recv()
            for k in range(bits):

                @pl.when(is_set[k])
                def _():
                    got = rc[k - 1, q0:q1] if k else rx0[q0:q1]
                    carry[k * nstate + n0 : k * nstate + n1, :] = got.reshape(
                        n1 - n0, feats
                    ).astype(BF16)

            held = [carry[k * nstate + n0 : k * nstate + n1, :] for k in range(bits)]
            terms = mm_nt(jnp.concatenate(held, axis=0), d_ref[...])
            total = grads[1, n0:n1, :]
            for k in range(bits):
                lam = wt_ref[low_bits + 1 + k : low_bits + 2 + k, :]
                total = total + terms[k * (n1 - n0) : (k + 1) * (n1 - n0), :] * lam
            grads[1, n0:n1, :] = total
            spread(1, g)

    def far_down(g, which):
        ending = which == 2
        q0, q1 = GROUPS[g]
        n0, n1 = q0 * rows_q, q1 * rows_q

        @pl.when(classes[which])
        def _():
            every = xb_all(q0, q1 - q0, g).wait_recv
            if ending:
                pl.when(mine[0])(every)
            elif split:
                pl.when(mine[0] | jnp.logical_not(beside))(every)
                given = sum(not splits_down(1, q) or q % 2 == 0 for q in range(q0, q1))
                pl.when(beside & mine[1])(xb_all(q0, given, g).wait_recv)
            else:
                every()
            held = (tot[q0:q1] + rxb[q0:q1]).reshape(n1 - n0, feats).astype(BF16)
            back[n0:n1, :] = held
            grads[0, n0:n1, :] = grads[0, n0:n1, :] + mm_nt(held, x_ref[...])
            spread(0, g)

    def halfway(array, g, which, turn=None):
        here = classes[which] if turn is None else classes[which] & (pair == turn)
        pl.when(here)(lambda: middle(array, g))

    def finish_y(n, which):
        @pl.when(classes[which])
        def _():
            for q in range(n * strips // 2, (n + 1) * strips // 2):
                cols = slice(q * WIDTH, (q + 1) * WIDTH)
                y_ref[:, cols] = (y_acc[:, cols] + mm(rise[...], carry[:, cols])).astype(BF16)

    def late_sends(q):
        pl.when(last & mine[0])(x0_copy(q).start)
        pl.when(last & mine[1])(xg_copy(q).start)

    def rises():
        c_f = c_ref[...].astype(F32)
        for k in range(bits):
            lam = w_ref[:, low_bits + 1 + k : low_bits + 2 + k]
            rise[:, k * nstate : (k + 1) * nstate] = (c_f * lam).astype(BF16)

    plan = []

    def put(time, name, step, *args):
        plan.append((time, len(plan), name, step, args))

    def rise_at(k, q):
        return (6.2 if k == 1 else 9.0 + 5.8 * (k - 2)) + BEAT * q

    def lead(q):
        n = TOP_SPLIT[0]
        return BEAT * q if q < n else BEAT * n + 0.4 * (q - n)

    def fall_at(k, q):
        return 10.2 + 3.6 * (top - k) + lead(q)

    for q in range(CHUNKS):
        for k in levels:
            put(rise_at(k, q), "source", source, k, q)
            put(fall_at(k, q), "pass_down", pass_down, k, q)
            if k > 1:
                put(rise_at(k, q) + 3.4, "relay_up", relay_up, k, q)
                put(6.4 + lead(q) if k == top else fall_at(k, q) - 1.4, "relay_down", relay_down, k, q)
            if splits_up(k, q):
                put(rise_at(k, q) + 3.6 + 0.1 * q, "gather", gather, k, q)
            if k < top:
                put(8.4 + 0.28 * q, "descend", descend, k, q)
            elif splits_down(k, q):
                put(6.9 + 0.2 * (q - TOP_SPLIT[0]), "descend", descend, k, q)
        if split:
            put(16.0 + 0.45 * q, "beside", beside_down, q)
        if q >= EARLY:
            put(8.0 + 0.95 * (q - EARLY), "late", late_sends, q)
    deeper = max(top - 2, 0)
    for which, times in enumerate((FIRST_AT, INNER_AT, LAST_AT)):
        ups, downs, up_halves, down_halves, ys = times
        later = 5.8 * deeper
        for g in range(len(GROUPS)):
            put(ups[g] + later, "far_up", far_up, g, which)
            put(downs[g] + later, "far_down", far_down, g, which)
            if g != final:
                put(up_halves[g] + later, "halfway", halfway, 1, g, which)
                if g == final - 1:
                    put(down_halves[g] + later, "halfway", halfway, 0, g, which, 0)
                    put(max(down_halves[g], downs[final]) + 0.1 + later, "halfway", halfway, 0, g, which, 1)
                else:
                    put(down_halves[g] + later, "halfway", halfway, 0, g, which)
        for n in range(2):
            put(ys[n] + later, "finish_y", finish_y, n, which)
    near = [(weigh, 0)]
    for i in range(1, blocks):
        near += [(weigh, i), (near_y, i - 1)]
    near += [(near_y, blocks - 1)] + [(near_dx, j) for j in range(blocks)]
    for n, (step, i) in enumerate(near):
        put(4.3 + 13.2 / len(near) * n, step.__name__, step, i)
    put(18.6, "rises", rises)
    for _, _, name, step, args in sorted(plan, key=lambda item: item[:2]):
        with scope(name + "_" + "_".join(str(a) for a in args)):
            step(*args)

    with scope("dx"):
        for q in range(strips):
            cols = slice(q * WIDTH, (q + 1) * WIDTH)
            dx_ref[:, cols] = (dx_acc[:, cols] + mm(b_ref[...], back[:, cols])).astype(BF16)
    def finish(array):
        parts = []
        for g in range(len(GROUPS)):
            rows = rows_of(g)
            if g == final:
                ahead, total = heads - 1, grads[array, rows, lanes_of(head)]
            else:
                ahead, total = max(ways - 1, 0), sums[0, array, rows]
            if ahead:
                given = hr.at[pl.ds(0, ahead), array, rows]
                remote(given, given, hd_s.at[0], hd_r.at[array, g], {"head": fellow}).wait_recv()
            for m in range(ahead):
                total = total + hr[m, array, rows]
            parts.append(total)
        (db_ref, dc_ref)[array][...] = jnp.concatenate(parts, axis=0).T

    for ending in range(2):

        @pl.when(last if ending else inner)
        def _():
            for array in (0, 1) if ending else (1, 0):
                with scope(f"heads_{array}_{ending}"):
                    finish(array)

    def sent(sem, n, condition):
        if n:
            held = s_buf.at[pl.ds(0, n)]
            pl.when(condition)(remote(held, held, sem, x0_r.at[0], {"ctx": partner}).wait_send)

    with scope("drain"):
        if ways:
            tail = hr.at[:, :, rows_of(final)]
            early = pl.ds(0, GROUPS[final][0] * rows_q)
            whole, rest = h1.at[:, :, early], hr.at[pl.ds(0, ways - 1), :, early]
            remote(tail, tail, hd_s.at[0], h1_r.at[0, 0], {"head": fellow}).wait_send()
            remote(whole, whole, hd_s.at[1], h1_r.at[0, 0], {"head": fellow}).wait_send()
            if ways > 1:
                remote(rest, rest, hd_s.at[2], h1_r.at[0, 0], {"head": fellow}).wait_send()
        if split:
            apart = jnp.logical_not(beside)
            sent(x0_s.at[0], CHUNKS, (inner & apart) | mine[0])
            sent(x0_s.at[0], owned(splits_up, 1, 0), beside & mine[1])
            sent(xb_s.at[0], CHUNKS, (inner & apart) | mine[1])
            sent(xb_s.at[0], owned(splits_down, 1, 0), beside & mine[0])
        else:
            sent(x0_s.at[0], CHUNKS, inner | mine[0])
            sent(xb_s.at[0], CHUNKS, inner | mine[1])
        for k in levels:
            for line in range(2):
                full = mine[line] & jnp.logical_not(beside)
                edge = mine[line] & beside
                sent(up_s.at[0], CHUNKS, low_top[k] & full)
                sent(up_s.at[0], owned(splits_up, k, line), low_top[k] & edge)
                sent(fw_s.at[k - 1], CHUNKS, relay[k] & full)
                sent(fw_s.at[k - 1], owned(splits_up, k, line), relay[k] & edge)
                sent(ga_s.at[k - 1], shared(splits_up, k, line), last & mine[line])
                sent(pr_s.at[k - 1], shared(splits_down, k, 1 - line), last & mine[line])
                sent(bk_s.at[k - 1], CHUNKS, is_set[k] & mine[line] & inner)
                sent(bk_s.at[k - 1], owned(splits_down, k, line), last & mine[line])


def write_out(*refs):
    copies = [pltpu.make_async_copy(refs[n], refs[n + 4], refs[8].at[n]) for n in range(4)]
    for copy in copies:
        copy.start()
    for copy in copies:
        copy.wait()


def local(x_in, b_in, c_in, d_out, table, level_index):
    toks, feats = x_in.shape
    nstate = b_in.shape[1]
    count, heads = lax.axis_size("ctx"), lax.axis_size("head")
    bits = count.bit_length() - 1
    strips = feats // WIDTH
    index = level_index.reshape(1, toks)
    rows = toks // heads
    ups = max(bits - 1, 1)
    others = max(heads - 1, 1)
    vmem = pl.BlockSpec(memory_space=pltpu.VMEM)
    hbm = pl.BlockSpec(memory_space=pltpu.HBM)
    dma = pltpu.SemaphoreType.DMA
    slab = (CHUNKS, nstate // CHUNKS, feats)
    results = pl.pallas_call(
        functools.partial(kernel, count, heads),
        out_shape=(
            pltpu.VMEM((toks, feats), BF16),
            pltpu.VMEM((toks, feats), BF16),
            pltpu.VMEM((rows, nstate), F32),
            pltpu.VMEM((rows, nstate), F32),
        ),
        in_specs=[hbm] * 6,
        out_specs=(vmem,) * 4,
        scratch_shapes=[
            pltpu.VMEM((toks, feats), BF16),
            pltpu.VMEM((toks, feats), BF16),
            pltpu.VMEM((toks, nstate), BF16),
            pltpu.VMEM((toks, nstate), BF16),
            pltpu.VMEM(table.shape, F32),
            pltpu.VMEM((1, toks), jnp.int32),
            pltpu.VMEM((table.shape[0], nstate), F32),
            pltpu.VMEM((toks, nstate), F32),
            pltpu.VMEM((nstate, toks), F32),
            pltpu.VMEM((nstate, toks), BF16),
            pltpu.VMEM((nstate, toks), BF16),
            pltpu.VMEM((toks, toks), BF16),
            pltpu.VMEM((toks, toks), BF16),
            pltpu.VMEM((toks, feats), F32),
            pltpu.VMEM((toks, feats), F32),
            pltpu.VMEM((2, nstate, toks), F32),
            pltpu.VMEM((toks, bits * nstate), BF16),
            pltpu.VMEM((bits * nstate, toks), BF16),
            pltpu.VMEM((bits * nstate, feats), BF16),
            pltpu.VMEM((nstate, feats), BF16),
            pltpu.VMEM(slab, F32),
            pltpu.VMEM((bits,) + slab, F32),
            pltpu.VMEM(slab, F32),
            pltpu.VMEM(slab, F32),
            pltpu.VMEM((ups,) + slab, F32),
            pltpu.VMEM((ups,) + slab, F32),
            pltpu.VMEM(slab, F32),
            pltpu.VMEM(slab, F32),
            pltpu.VMEM(slab, F32),
            pltpu.VMEM((others, 2, nstate, rows), F32),
            pltpu.VMEM((max(heads // 2, 1), 2, nstate, rows), F32),
            pltpu.VMEM((max(heads // 2, 1), 2, nstate, rows), F32),
            dma((4,)),
            dma((feats // WIDTH,)),
            dma((1,)),
            dma((1,)),
            dma((CHUNKS,)),
            dma((1,)),
            dma((ups,)),
            dma((ups, CHUNKS)),
            dma((ups,)),
            dma((ups,)),
            dma((ups,)),
            dma((max(ups - 1, 1), CHUNKS if ups > 1 else 1)),
            dma((1,)),
            dma((len(GROUPS),)),
            dma((3,)),
            dma((2, len(GROUPS))),
            dma((2, len(GROUPS) - 1)),
        ],
        compiler_params=pltpu.CompilerParams(
            collective_id=0,
            has_side_effects=True,
            vmem_limit_bytes=VMEM_BYTES - 4 * toks * feats - 8 * rows * nstate - SPARE,
        ),
    )(x_in, b_in, c_in, d_out, table, index)
    return pl.pallas_call(
        write_out,
        out_shape=tuple(jax.ShapeDtypeStruct(r.shape, r.dtype) for r in results),
        in_specs=[vmem] * 4,
        out_specs=(hbm,) * 4,
        scratch_shapes=[dma((4,))],
        compiler_params=pltpu.CompilerParams(vmem_limit_bytes=1024 * 1024),
    )(*results)


def solution(mesh):
    return jax.shard_map(
        local,
        mesh=mesh,
        in_specs=(
            P("ctx", "head"),
            P("ctx", None),
            P("ctx", None),
            P("ctx", "head"),
            P(),
            P("ctx"),
        ),
        out_specs=(
            P("ctx", "head"),
            P("ctx", "head"),
            P(("ctx", "head"), None),
            P(("ctx", "head"), None),
        ),
        check_vma=False,
    )
```

```python
import contextlib
import functools

import jax
import jax.numpy as jnp
from jax import lax
from jax.experimental import pallas as pl
from jax.experimental.pallas import tpu as pltpu
from jax.sharding import PartitionSpec as P

F32 = jnp.float32
BF16 = jnp.bfloat16
MESH = pl.DeviceIdType.MESH
TILE = 256
WIDTH = 256
CHUNKS = 16
GROUPS = ((0, 10), (10, 14), (14, 16))
FIRST_AT = ((13.3, 16.6, 18.4), (22.9, 25.6, 27.0), (16.9, 19.9), (24.9, 27.1), (19.3, 20.7))
INNER_AT = ((20.2, 22.3, 23.5), (24.0, 26.5, 28.0), (23.0, 25.2), (26.3, 28.1), (24.4, 25.5))
LAST_AT = ((23.2, 26.2, 27.2), (21.9, 22.9, 24.9), (25.6, 28.2), (24.6, 25.8), (28.0, 28.6))
EARLY = 2
BEAT = 0.7
WAIT_FIRST = 4.0
CROSS_LATE = 0.0
UP_SPLIT = range(7, 15)
TOP_UP_SPLIT = (2, 3, 4, 5)
FIRST_SPLIT = ()
DOWN_SPLIT = range(1, 8)
TOP_SPLIT = range(8, 16)
VMEM_BYTES = 67043328
SPARE = 16384
EXTRA = 1024 * 1024


def scope(name):
    return contextlib.nullcontext()


def mm(a, b):
    return jnp.dot(a, b, preferred_element_type=F32)


def mm_tn(a, b):
    return lax.dot_general(a, b, (((0,), (0,)), ((), ())), preferred_element_type=F32)


def mm_nt(a, b):
    return lax.dot_general(a, b, (((1,), (1,)), ((), ())), preferred_element_type=F32)


def bit_count(values, bits):
    counted = jnp.zeros(values.shape, jnp.int32)
    for digit_no in range(bits):
        counted = counted + (values >= 1 << digit_no).astype(jnp.int32)
    return counted


def kernel(
    count,
    heads,
    x_hbm,
    b_hbm,
    c_hbm,
    d_hbm,
    table_hbm,
    index_hbm,
    y_ref,
    dx_ref,
    sums,
    hr,
    x_ref,
    d_ref,
    b_ref,
    c_ref,
    table_ref,
    index_ref,
    wide_table,
    w_ref,
    wt_ref,
    bt_ref,
    ct_ref,
    mix,
    d_mix,
    y_acc,
    dx_acc,
    grads,
    rise,
    rise_t,
    carry,
    back,
    s_buf,
    g_buf,
    rx0,
    up,
    rc,
    rb,
    tot,
    xb,
    rxb,
    h1,
    small_sem,
    x_sem,
    d_sem,
    x0_s,
    x0_r,
    up_s,
    fw_s,
    rc_r,
    ga_s,
    pr_s,
    bk_s,
    rb_r,
    xb_s,
    xb_r,
    hd_s,
    hd_r,
    h1_r,
):
    bits = count.bit_length() - 1
    top = bits - 1
    toks, feats = x_ref.shape
    nstate = b_ref.shape[1]
    rows_q = nstate // CHUNKS
    blocks = toks // TILE
    part = toks // heads
    tile_bits = TILE.bit_length() - 1
    low_bits = toks.bit_length() - 1
    me = lax.axis_index("ctx")
    head = lax.axis_index("head")
    par = me % 2
    col = me // 2
    levels = range(1, bits)
    columns = count // 2
    split = bits >= 3
    is_set = {k: (me // (1 << k)) % 2 == 1 for k in range(bits)}
    low_top = {k: col % (1 << k) == (1 << (k - 1)) - 1 for k in levels}
    up_top = {k: col % (1 << k) == (1 << k) - 1 for k in levels}
    relay = {k: is_set[k] & jnp.logical_not(up_top[k]) for k in levels}
    last = col == columns - 1
    inner = jnp.logical_not(last)
    beside = col == columns - 2
    mine = (par == 0, par == 1)
    partner = me + 1 - 2 * par

    def splits_up(k, q):
        return split and q in (UP_SPLIT if k < top else TOP_UP_SPLIT)

    def splits_first(q):
        return split and q in FIRST_SPLIT

    def splits_down(k, q):
        return split and q in (DOWN_SPLIT if k < top else TOP_SPLIT)

    def owned(splits, k, line):
        return sum(not splits(k, q) or q % 2 == line for q in range(CHUNKS))

    def shared(splits, k, line):
        return sum(splits(k, q) and q % 2 == line for q in range(CHUNKS))

    first, second = col == 0, col == 1
    classes = (first & inner, inner & jnp.logical_not(first), last)

    def carried_up(k, q):
        return jnp.logical_not(beside) | mine[q % 2] if splits_up(k, q) else None

    def carried_down(k, q):
        return jnp.logical_not(beside) | mine[q % 2] if splits_down(k, q) else None

    def when(condition, body):
        if condition is None:
            body()
        else:
            pl.when(condition)(body)

    strips = feats // WIDTH
    loads = [
        pltpu.make_async_copy(hbm, vmem, small_sem.at[n])
        for n, (hbm, vmem) in enumerate(
            (
                (table_hbm, table_ref),
                (index_hbm, index_ref),
                (c_hbm, c_ref),
                (b_hbm, b_ref),
            )
        )
    ]

    def fill_x(n):
        cols = pl.ds(n * WIDTH, WIDTH)
        return pltpu.make_async_copy(x_hbm.at[:, cols], x_ref.at[:, cols], x_sem.at[0])

    fill_d = pltpu.make_async_copy(d_hbm, d_ref, d_sem.at[0])
    def load_states():
        loads[3].start()
        for n in range(strips):
            fill_x(n).start()

    def load_weights():
        for load in loads[:3]:
            load.start()

    @pl.when(inner)
    def _():
        load_states()
        load_weights()

    @pl.when(last)
    def _():
        load_weights()
        fill_d.start()

    barrier = pltpu.get_barrier_semaphore()
    pl.semaphore_signal(barrier, inc=1, device_id={"ctx": partner}, device_id_type=MESH)

    @pl.when(col > 0)
    def _():
        pl.semaphore_signal(barrier, inc=1, device_id={"ctx": me - 2}, device_id_type=MESH)

    @pl.when(inner)
    def _():
        pl.semaphore_signal(barrier, inc=1, device_id={"ctx": me + 2}, device_id_type=MESH)

    peers = [(head + m) % heads for m in range(1, heads)]
    for peer in peers:
        pl.semaphore_signal(barrier, inc=1, device_id={"head": peer}, device_id_type=MESH)

    def remote(src, dst, ssem, rsem, device):
        return pltpu.make_async_remote_copy(
            src_ref=src,
            dst_ref=dst,
            send_sem=ssem,
            recv_sem=rsem,
            device_id=device,
            device_id_type=MESH,
        )

    def x0_copy(q):
        return remote(s_buf.at[q], rx0.at[q], x0_s.at[0], x0_r.at[q], {"ctx": partner})

    def fall_sem(k, q):
        return rb_r.at[k - 2, q] if k > 1 else rc_r.at[0, q]

    def up_copy(k, q):
        return remote(up.at[q], rc.at[k - 1, q], up_s.at[0], rc_r.at[k - 1, q], {"ctx": me + 2})

    def forward_copy(k, q):
        held = rc.at[k - 1, q]
        return remote(held, held, fw_s.at[k - 1], rc_r.at[k - 1, q], {"ctx": me + 2})

    def gather_copy(k, q):
        held = rc.at[k - 1, q]
        return remote(held, held, ga_s.at[k - 1], rc_r.at[k - 1, q], {"ctx": partner})

    def pre_copy(k, q):
        return remote(
            g_buf.at[k, q], rb.at[k - 1, q], pr_s.at[k - 1], fall_sem(k if k > 1 else top, q), {"ctx": partner}
        )

    def back_copy(k, q):
        return remote(
            g_buf.at[k, q], rb.at[k - 1, q], bk_s.at[k - 1], fall_sem(k, q), {"ctx": me - 2}
        )

    def group_of(q):
        return next(g for g, (q0, q1) in enumerate(GROUPS) if q0 <= q < q1)

    def xb_copy(q):
        return remote(xb.at[q], rxb.at[q], xb_s.at[0], xb_r.at[group_of(q)], {"ctx": partner})

    def xg_copy(q):
        return remote(
            g_buf.at[0, q], rxb.at[q], xb_s.at[0], xb_r.at[group_of(q)], {"ctx": partner}
        )

    def xb_all(q0, n, g):
        held = pl.ds(q0, n)
        return remote(xb.at[held], rxb.at[held], xb_s.at[0], xb_r.at[g], {"ctx": partner})

    def states():
        with scope("b"):
            b_t = b_ref[...].astype(F32).T.astype(BF16)
            bt_ref[...] = b_t
        with scope("xw"):
            pltpu.make_async_copy(x_hbm, x_ref, x_sem.at[0]).wait()
        with scope("s"):
            for q in range(strips):
                cols = slice(q * WIDTH, (q + 1) * WIDTH)
                s_buf[:, :, cols] = mm(b_t, x_ref[:, cols]).reshape(CHUNKS, rows_q, WIDTH)

    def weights():
        wide_table[...] = jnp.zeros_like(wide_table)
        wide_table[:, : table_ref.shape[1]] = table_ref[...]
        hot = (
            lax.broadcasted_iota(jnp.int32, (table_ref.shape[0], toks), 0) == index_ref[...]
        ).astype(F32)
        w_t = lax.dot_general(
            wide_table[...],
            hot,
            (((0,), (0,)), ((), ())),
            preferred_element_type=F32,
            precision=lax.Precision.HIGHEST,
        )
        wt_ref[...] = w_t
        c_t = c_ref[...].astype(F32).T
        ct_ref[...] = c_t.astype(BF16)
        for k in range(bits):
            lam_t = w_t[low_bits + 1 + k : low_bits + 2 + k, :]
            rise_t[k * nstate : (k + 1) * nstate, :] = (c_t * lam_t).astype(BF16)

    def meet():
        ends = (col > 0).astype(jnp.int32) + inner.astype(jnp.int32)
        pl.semaphore_wait(barrier, heads + ends)

    @pl.when(inner)
    def _():
        with scope("bw"):
            loads[3].wait()
        fill_d.start()
        states()
        with scope("barrier"):
            meet()
        for q in range(CHUNKS):
            spared = []
            if splits_up(1, q) and q % 2:
                spared.append(beside & mine[1])
            if splits_first(q):
                spared.append(first & mine[1])
            when(jnp.logical_not(functools.reduce(jnp.logical_or, spared)) if spared else None, x0_copy(q).start)
        with scope("tw"):
            for load in loads[:3]:
                load.wait()
        with scope("w"):
            weights()

    @pl.when(last)
    def _():
        with scope("tw"):
            for load in loads[:3]:
                load.wait()
        load_states()
        with scope("w"):
            weights()

    with scope("dw"):
        fill_d.wait()
    for k in reversed(range(bits)):
        with scope(f"g{k}"):

            @pl.when(is_set[k])
            def _():
                for q in range(strips):
                    cols = slice(q * WIDTH, (q + 1) * WIDTH)
                    part_g = mm(rise_t[k * nstate : (k + 1) * nstate, :], d_ref[:, cols])
                    g_buf[k, :, :, cols] = part_g.reshape(CHUNKS, rows_q, WIDTH)

        @pl.when(last)
        def _():
            if k == top:
                meet()
            for q in range(CHUNKS if k else 0):
                if splits_down(k, q):
                    pl.when(mine[1 - q % 2])(pre_copy(k, q).start)
                elif k == top:
                    back_copy(k, q).start()
            if k == 0:
                for q in range(EARLY):
                    pl.when(mine[1])(xg_copy(q).start)

        if k == 0:

            @pl.when(beside & mine[1])
            def _():
                for q in range(CHUNKS):
                    if splits_down(1, q) and q % 2 == 0:
                        xg_copy(q).start()

    @pl.when(last)
    def _():
        loads[3].wait()
        states()
        for q in range(EARLY):
            pl.when(mine[0])(x0_copy(q).start)

    with scope("w2"):
        w_ref[...] = wt_ref[...].T
        carry[...] = jnp.zeros_like(carry)

        @pl.when(last)
        def _():
            tot[...] = jnp.zeros_like(tot)

        pl.when(last & mine[1])(lambda: rxb.__setitem__(..., jnp.zeros_like(rxb)))
        if split:

            @pl.when(beside & mine[1])
            def _():
                for q in range(CHUNKS):
                    if splits_down(1, q) and q % 2:
                        rxb[q] = jnp.zeros_like(rxb[q])

    half = TILE // 2

    def diagonal(w_rows):
        row = lax.broadcasted_iota(jnp.int32, (half, half), 0)
        at = lax.broadcasted_iota(jnp.int32, (half, half), 1)
        differ = row ^ at
        weight = jnp.broadcast_to(w_rows[:, 0:1], (half, half))
        for n in range(tile_bits - 1):
            weight = jnp.where(differ >= 1 << n, w_rows[:, n + 1 : n + 2], weight)
        return jnp.where(at <= row, weight, 0.0)

    def weigh_diagonal(i):
        rows = slice(i * TILE, (i + 1) * TILE)
        w_rows = w_ref[rows, :]
        upper, lower = w_rows[:half], w_rows[half:]
        side = jnp.broadcast_to(lower[:, tile_bits : tile_bits + 1], (half, half))
        weight = jnp.concatenate(
            [
                jnp.concatenate([diagonal(upper), jnp.zeros((half, half), F32)], axis=1),
                jnp.concatenate([side, diagonal(lower)], axis=1),
            ],
            axis=0,
        )
        mix[rows, rows] = (mm_nt(c_ref[rows, :], b_ref[rows, :]) * weight).astype(BF16)
        d_mix[rows, rows] = (mm_nt(d_ref[rows, :], x_ref[rows, :]) * weight).astype(BF16)

    def weigh(i):
        rows = slice(i * TILE, (i + 1) * TILE)
        w_rows = w_ref[rows, :]
        c_i, d_i = c_ref[rows, :], d_ref[rows, :]
        for j in range(i):
            cols = slice(j * TILE, (j + 1) * TILE)
            level = tile_bits + (i ^ j).bit_length()
            factor = w_rows[:, level : level + 1]
            mix[rows, cols] = (mm_nt(c_i, b_ref[cols, :]) * factor).astype(BF16)
            d_mix[rows, cols] = (mm_nt(d_i, x_ref[cols, :]) * factor).astype(BF16)

    def near_y(i, n0, n1):
        rows = slice(i * TILE, (i + 1) * TILE)
        seen = slice(0, (i + 1) * TILE)
        part_y = slice(n0 * feats // 2, n1 * feats // 2)
        y_acc[rows, part_y] = mm(mix[rows, seen], x_ref[seen, part_y])
        if n0 == 0:
            grads[1, :, rows] = mm_nt(bt_ref[:, seen], d_mix[rows, seen])

    def near_dx(j, n0, n1):
        cols = slice(j * TILE, (j + 1) * TILE)
        seen = slice(j * TILE, toks)
        part_x = slice(n0 * feats // 2, n1 * feats // 2)
        dx_acc[cols, part_x] = mm_tn(mix[seen, cols], d_ref[seen, part_x])
        if n0 == 0:
            grads[0, :, cols] = mm(ct_ref[:, seen], d_mix[seen, cols])

    def source(k, q, line=None):
        here = low_top[k]
        if k == 1 and splits_up(1, q):
            here = here & jnp.logical_not(beside & mine[1 - q % 2])
            if q % 2 == 0:
                pl.when(beside & mine[1])(x0_copy(q).wait_recv)
        if k == 1 and splits_first(q):
            here = here & jnp.logical_not(first & mine[0])
        if line is not None:
            here = here & mine[line]

        @pl.when(here)
        def _():
            x0_copy(q).wait_recv()
            group = s_buf[q] + rx0[q]
            for j in range(1, k):
                up_copy(j, q).wait_recv()
                if j == 1 and line == 1:
                    pl.when(second)(gather_copy(1, q).start)
                group = group + rc[j - 1, q]
            up[q] = group
            up_copy(k, q).start()

    def relay_up(k, q, line=None):
        @pl.when(relay[k] if line is None else relay[k] & mine[line])
        def _():
            up_copy(k, q).wait_recv()
            when(carried_up(k, q), forward_copy(k, q).start)

    def gather(k, q):
        @pl.when(last & mine[q % 2])
        def _():
            up_copy(k, q).wait_recv()
            gather_copy(k, q).start()

    def descend(k, q):
        if splits_down(k, q):

            @pl.when(last & mine[q % 2])
            def _():
                pre_copy(k, q).wait_recv()
                g_buf[k, q] = g_buf[k, q] + rb[k - 1, q]
                back_copy(k, q).start()

        else:
            pl.when(last)(back_copy(k, q).start)

    def relay_down(k, q):
        @pl.when(relay[k])
        def _():
            def add():
                back_copy(k, q).wait_recv()
                g_buf[k, q] = g_buf[k, q] + rb[k - 1, q]

            when(carried_down(k, q), add)
            back_copy(k, q).start()

    def cross(q):
        @pl.when(mine[1])
        def _():
            xb[q] = tot[q] + g_buf[0, q]

        @pl.when(mine[0])
        def _():
            xb[q] = tot[q]

    def pass_down(k, q):
        here = low_top[k] & jnp.logical_not(beside) if split else low_top[k]

        @pl.when(here)
        def _():
            back_copy(k, q).wait_recv()
            got = rb[k - 1, q]
            tot[q] = got
            for j in range(1, k):
                g_buf[j, q] = g_buf[j, q] + got
                back_copy(j, q).start()
            if k == 2 and split:
                pl.when(jnp.logical_not(second))(lambda: send_cross(q))
            else:
                send_cross(q)

    def send_cross(q):
        cross(q)
        xb_copy(q).start()

    def cross_late(q):
        pl.when(second)(lambda: send_cross(q))

    def beside_down(q):
        def own():
            back_copy(1, q).wait_recv()
            tot[q] = rb[0, q]
            cross(q)
            xb_copy(q).start()

        if splits_down(1, q):
            pl.when(beside & mine[q % 2])(own)

            @pl.when(beside & mine[1 - q % 2])
            def _():
                tot[q] = jnp.zeros_like(tot[q])

        else:
            pl.when(beside)(own)

    final = len(GROUPS) - 1
    pair = head % 2
    fellow = head + 1 - 2 * pair
    ways = heads // 2

    def lanes_of(h):
        return pl.ds(pl.multiple_of(h * part, part), part)

    def rows_of(g):
        return pl.ds(GROUPS[g][0] * rows_q, (GROUPS[g][1] - GROUPS[g][0]) * rows_q)

    def spread(array, g):
        rows = rows_of(g)
        if g == final:
            sums[0, array, rows] = grads[array, rows, lanes_of(head)]
            for m, peer in enumerate(peers):
                remote(
                    grads.at[array, rows, lanes_of(peer)],
                    hr.at[m, array, rows],
                    hd_s.at[0],
                    hd_r.at[array, g],
                    {"head": peer},
                ).start()
        else:
            for j in range(ways):
                remote(
                    grads.at[array, rows, lanes_of(2 * j + 1 - pair)],
                    h1.at[j, array, rows],
                    hd_s.at[1],
                    h1_r.at[array, g],
                    {"head": fellow},
                ).start()

    def middle(array, g):
        rows = rows_of(g)
        if ways:
            given = h1.at[:, array, rows]
            remote(given, given, hd_s.at[1], h1_r.at[array, g], {"head": fellow}).wait_recv()
        for m in range(max(ways, 1)):
            j = (head // 2 + m) % max(ways, 1)
            total = grads[array, rows, lanes_of(2 * j + pair)]
            if ways:
                total = total + h1[j, array, rows]
            sums[m, array, rows] = total
            if m:
                remote(
                    sums.at[m, array, rows],
                    hr.at[m - 1, array, rows],
                    hd_s.at[2],
                    hd_r.at[array, g],
                    {"head": 2 * j + pair},
                ).start()

    def far_up(g, which):
        ending = which == 2
        q0, q1 = GROUPS[g]
        n0, n1 = q0 * rows_q, q1 * rows_q

        @pl.when(classes[which])
        def _():
            for q in range(q0, q1) if ending else ():
                pl.when(mine[1])(x0_copy(q).wait_recv)
                for k in levels:
                    if splits_up(k, q):
                        pl.when(mine[1 - q % 2])(gather_copy(k, q).wait_recv)
                    else:
                        up_copy(k, q).wait_recv()
            for k in range(bits):

                @pl.when(is_set[k])
                def _():
                    got = rc[k - 1, q0:q1] if k else rx0[q0:q1]
                    carry[k * nstate + n0 : k * nstate + n1, :] = got.reshape(
                        n1 - n0, feats
                    ).astype(BF16)

            held = [carry[k * nstate + n0 : k * nstate + n1, :] for k in range(bits)]
            terms = mm_nt(jnp.concatenate(held, axis=0), d_ref[...])
            total = grads[1, n0:n1, :]
            for k in range(bits):
                lam = wt_ref[low_bits + 1 + k : low_bits + 2 + k, :]
                total = total + terms[k * (n1 - n0) : (k + 1) * (n1 - n0), :] * lam
            grads[1, n0:n1, :] = total
            spread(1, g)

    def far_down(g, which):
        ending = which == 2
        q0, q1 = GROUPS[g]
        n0, n1 = q0 * rows_q, q1 * rows_q

        @pl.when(classes[which])
        def _():
            every = xb_all(q0, q1 - q0, g).wait_recv
            if ending:
                pl.when(mine[0])(every)
            elif split:
                pl.when(mine[0] | jnp.logical_not(beside))(every)
                given = sum(not splits_down(1, q) or q % 2 == 0 for q in range(q0, q1))
                pl.when(beside & mine[1])(xb_all(q0, given, g).wait_recv)
            else:
                every()
            held = (tot[q0:q1] + rxb[q0:q1]).reshape(n1 - n0, feats).astype(BF16)
            back[n0:n1, :] = held
            grads[0, n0:n1, :] = grads[0, n0:n1, :] + mm_nt(held, x_ref[...])
            spread(0, g)

    def halfway(array, g, which, turn=None):
        here = classes[which] if turn is None else classes[which] & (pair == turn)
        pl.when(here)(lambda: middle(array, g))

    def finish_y(n, which):
        @pl.when(classes[which])
        def _():
            for q in range(n * strips // 2, (n + 1) * strips // 2):
                cols = slice(q * WIDTH, (q + 1) * WIDTH)
                y_ref[:, cols] = (y_acc[:, cols] + mm(rise[...], carry[:, cols])).astype(BF16)

    def late_sends(q):
        pl.when(last & mine[0])(x0_copy(q).start)
        pl.when(last & mine[1])(xg_copy(q).start)

    def rises():
        c_f = c_ref[...].astype(F32)
        for k in range(bits):
            lam = w_ref[:, low_bits + 1 + k : low_bits + 2 + k]
            rise[:, k * nstate : (k + 1) * nstate] = (c_f * lam).astype(BF16)

    plan = []

    def put(time, name, step, *args):
        plan.append((time, len(plan), name, step, args))

    def rise_at(k, q):
        return (6.2 if k == 1 else 9.0 + 5.8 * (k - 2)) + BEAT * q

    def lead(q):
        n = TOP_SPLIT[0]
        return BEAT * q if q < n else BEAT * n + 0.4 * (q - n)

    def fall_at(k, q):
        return 10.2 + 3.6 * (top - k) + lead(q)

    for q in range(CHUNKS):
        for k in levels:
            apart = 2 if k == 2 and splits_first(q) else 0
            for line in range(apart):
                put(rise_at(k, q) + WAIT_FIRST * (1 - line), "source", source, k, q, line)
                put(rise_at(k, q) + 3.4 + WAIT_FIRST * (1 - line), "relay_up", relay_up, k, q, line)
            if not apart:
                put(rise_at(k, q), "source", source, k, q)
            put(fall_at(k, q), "pass_down", pass_down, k, q)
            if k > 1:
                if not apart:
                    put(rise_at(k, q) + 3.4, "relay_up", relay_up, k, q)
                put(6.4 + lead(q) if k == top else fall_at(k, q) - 1.4, "relay_down", relay_down, k, q)
            if splits_up(k, q):
                put(rise_at(k, q) + (3.6 + 0.1 * q if k < top else 6.6), "gather", gather, k, q)
            if k < top:
                put(8.8 + 0.35 * q, "descend", descend, k, q)
            elif splits_down(k, q):
                put(6.2 + 0.3 * (q - TOP_SPLIT[0]), "descend", descend, k, q)
        if split:
            put(fall_at(2, q) + CROSS_LATE, "cross", cross_late, q)
            put(15.0 + 0.45 * q + 0.23 * max(q - 7, 0), "beside", beside_down, q)
        if q >= EARLY:
            put(8.0 + 0.95 * (q - EARLY), "late", late_sends, q)
    deeper = max(top - 2, 0)
    for which, times in enumerate((FIRST_AT, INNER_AT, LAST_AT)):
        ups, downs, up_halves, down_halves, ys = times
        later = 5.8 * deeper
        for g in range(len(GROUPS)):
            put(ups[g] + later, "far_up", far_up, g, which)
            put(downs[g] + later, "far_down", far_down, g, which)
            if g != final:
                put(up_halves[g] + later, "halfway", halfway, 1, g, which)
                if g + 1 < final:
                    put(down_halves[g] + later, "halfway", halfway, 0, g, which, 0)
                    put(max(down_halves[g], downs[g + 1]) + 0.1 + later, "halfway", halfway, 0, g, which, 1)
                else:
                    put(down_halves[g] + later, "halfway", halfway, 0, g, which)
        for n in range(2):
            put(ys[n] + later, "finish_y", finish_y, n, which)
    def pieces(step, i, long):
        return [(step, i, 0, 1), (step, i, 1, 2)] if long else [(step, i, 0, 2)]

    near = [(weigh_diagonal, 0)]
    for i in range(1, blocks):
        near += [(weigh_diagonal, i), (weigh, i)] + pieces(near_y, i - 1, i > blocks // 2)
    near += pieces(near_y, blocks - 1, True)
    for j in range(blocks):
        near += pieces(near_dx, j, j < blocks // 2)
    for n, (step, *args) in enumerate(near):
        put(4.1 + 13.0 / len(near) * n, step.__name__, step, *args)
    put(18.6, "rises", rises)
    for _, _, name, step, args in sorted(plan, key=lambda item: item[:2]):
        with scope(name + "_" + "_".join(str(a) for a in args)):
            step(*args)

    with scope("dx"):
        for q in range(strips):
            cols = slice(q * WIDTH, (q + 1) * WIDTH)
            dx_ref[:, cols] = (dx_acc[:, cols] + mm(b_ref[...], back[:, cols])).astype(BF16)
    with scope("heads"):
        for array in range(2):
            for g in range(len(GROUPS)):
                ahead = heads - 1 if g == final else max(ways - 1, 0)
                if ahead:
                    given = hr.at[pl.ds(0, ahead), array, rows_of(g)]
                    remote(given, given, hd_s.at[0], hd_r.at[array, g], {"head": fellow}).wait_recv()

    def sent(sem, n, condition):
        if n:
            held = s_buf.at[pl.ds(0, n)]
            pl.when(condition)(remote(held, held, sem, x0_r.at[0], {"ctx": partner}).wait_send)

    with scope("drain"):
        if ways:
            tail = hr.at[:, :, rows_of(final)]
            early = pl.ds(0, GROUPS[final][0] * rows_q)
            whole, rest = h1.at[:, :, early], hr.at[pl.ds(0, ways - 1), :, early]
            remote(tail, tail, hd_s.at[0], h1_r.at[0, 0], {"head": fellow}).wait_send()
            remote(whole, whole, hd_s.at[1], h1_r.at[0, 0], {"head": fellow}).wait_send()
            if ways > 1:
                remote(rest, rest, hd_s.at[2], h1_r.at[0, 0], {"head": fellow}).wait_send()
        if split:
            apart = jnp.logical_not(beside)
            lesser = sum(splits_first(q) for q in range(CHUNKS))
            sent(x0_s.at[0], CHUNKS, mine[0] | (inner & apart & jnp.logical_not(first)))
            sent(x0_s.at[0], CHUNKS - lesser, first & mine[1])
            sent(up_s.at[0], CHUNKS - lesser, first & mine[0])
            sent(ga_s.at[0], lesser, second & mine[1])
            sent(x0_s.at[0], owned(splits_up, 1, 0), beside & mine[1])
            sent(xb_s.at[0], CHUNKS, (inner & apart) | mine[1])
            sent(xb_s.at[0], owned(splits_down, 1, 0), beside & mine[0])
        else:
            sent(x0_s.at[0], CHUNKS, inner | mine[0])
            sent(xb_s.at[0], CHUNKS, inner | mine[1])
        for k in levels:
            for line in range(2):
                full = mine[line] & jnp.logical_not(beside)
                edge = mine[line] & beside
                most = full & jnp.logical_not(first) if split and k == 1 and line == 0 else full
                sent(up_s.at[0], CHUNKS, low_top[k] & most)
                sent(up_s.at[0], owned(splits_up, k, line), low_top[k] & edge)
                sent(fw_s.at[k - 1], CHUNKS, relay[k] & full)
                sent(fw_s.at[k - 1], owned(splits_up, k, line), relay[k] & edge)
                sent(ga_s.at[k - 1], shared(splits_up, k, line), last & mine[line])
                sent(pr_s.at[k - 1], shared(splits_down, k, 1 - line), last & mine[line])
                sent(bk_s.at[k - 1], CHUNKS, is_set[k] & mine[line] & inner)
                sent(bk_s.at[k - 1], owned(splits_down, k, line), last & mine[line])


def write_out(heads, y_ref, dx_ref, sums, hr, y_hbm, dx_hbm, db_hbm, dc_hbm, db_ref, dc_ref, sem):
    copies = [
        pltpu.make_async_copy(src, dst, sem.at[n])
        for n, (src, dst) in enumerate(
            ((y_ref, y_hbm), (dx_ref, dx_hbm), (dc_ref, dc_hbm), (db_ref, db_hbm))
        )
    ]
    copies[0].start()
    copies[1].start()
    nstate = sums.shape[2]
    edge = GROUPS[-1][0] * (nstate // CHUNKS)
    for array, ref, copy in ((1, dc_ref, copies[2]), (0, db_ref, copies[3])):
        early, tail = sums[0, array, :edge], sums[0, array, edge:]
        for m in range(heads // 2 - 1):
            early = early + hr[m, array, :edge]
        for m in range(heads - 1):
            tail = tail + hr[m, array, edge:]
        ref[...] = jnp.concatenate([early, tail], axis=0).T
        copy.start()
    for copy in copies:
        copy.wait()


def local(x_in, b_in, c_in, d_out, table, level_index):
    toks, feats = x_in.shape
    nstate = b_in.shape[1]
    count, heads = lax.axis_size("ctx"), lax.axis_size("head")
    bits = count.bit_length() - 1
    strips = feats // WIDTH
    index = level_index.reshape(1, toks)
    rows = toks // heads
    ups = max(bits - 1, 1)
    others = max(heads - 1, 1)
    vmem = pl.BlockSpec(memory_space=pltpu.VMEM)
    hbm = pl.BlockSpec(memory_space=pltpu.HBM)
    dma = pltpu.SemaphoreType.DMA
    slab = (CHUNKS, nstate // CHUNKS, feats)
    results = pl.pallas_call(
        functools.partial(kernel, count, heads),
        out_shape=(
            pltpu.VMEM((toks, feats), BF16),
            pltpu.VMEM((toks, feats), BF16),
            pltpu.VMEM((max(heads // 2, 1), 2, nstate, rows), F32),
            pltpu.VMEM((others, 2, nstate, rows), F32),
        ),
        in_specs=[hbm] * 6,
        out_specs=(vmem,) * 4,
        scratch_shapes=[
            pltpu.VMEM((toks, feats), BF16),
            pltpu.VMEM((toks, feats), BF16),
            pltpu.VMEM((toks, nstate), BF16),
            pltpu.VMEM((toks, nstate), BF16),
            pltpu.VMEM(table.shape, F32),
            pltpu.VMEM((1, toks), jnp.int32),
            pltpu.VMEM((table.shape[0], nstate), F32),
            pltpu.VMEM((toks, nstate), F32),
            pltpu.VMEM((nstate, toks), F32),
            pltpu.VMEM((nstate, toks), BF16),
            pltpu.VMEM((nstate, toks), BF16),
            pltpu.VMEM((toks, toks), BF16),
            pltpu.VMEM((toks, toks), BF16),
            pltpu.VMEM((toks, feats), F32),
            pltpu.VMEM((toks, feats), F32),
            pltpu.VMEM((2, nstate, toks), F32),
            pltpu.VMEM((toks, bits * nstate), BF16),
            pltpu.VMEM((bits * nstate, toks), BF16),
            pltpu.VMEM((bits * nstate, feats), BF16),
            pltpu.VMEM((nstate, feats), BF16),
            pltpu.VMEM(slab, F32),
            pltpu.VMEM((bits,) + slab, F32),
            pltpu.VMEM(slab, F32),
            pltpu.VMEM(slab, F32),
            pltpu.VMEM((ups,) + slab, F32),
            pltpu.VMEM((ups,) + slab, F32),
            pltpu.VMEM(slab, F32),
            pltpu.VMEM(slab, F32),
            pltpu.VMEM(slab, F32),
            pltpu.VMEM((max(heads // 2, 1), 2, nstate, rows), F32),
            dma((4,)),
            dma((1,)),
            dma((1,)),
            dma((1,)),
            dma((CHUNKS,)),
            dma((1,)),
            dma((ups,)),
            dma((ups, CHUNKS)),
            dma((ups,)),
            dma((ups,)),
            dma((ups,)),
            dma((max(ups - 1, 1), CHUNKS if ups > 1 else 1)),
            dma((1,)),
            dma((len(GROUPS),)),
            dma((3,)),
            dma((2, len(GROUPS))),
            dma((2, len(GROUPS) - 1)),
        ],
        compiler_params=pltpu.CompilerParams(
            collective_id=0,
            has_side_effects=True,
            vmem_limit_bytes=VMEM_BYTES - 4 * toks * feats - 8 * (max(heads // 2, 1) + others) * rows * nstate - SPARE - EXTRA,
        ),
    )(x_in, b_in, c_in, d_out, table, index)
    slices = jax.ShapeDtypeStruct((rows, nstate), F32)
    wholes = jax.ShapeDtypeStruct((toks, feats), BF16)
    return pl.pallas_call(
        functools.partial(write_out, heads),
        out_shape=(wholes, wholes, slices, slices),
        in_specs=[vmem] * 4,
        out_specs=(hbm,) * 4,
        scratch_shapes=[
            pltpu.VMEM((rows, nstate), F32),
            pltpu.VMEM((rows, nstate), F32),
            dma((4,)),
        ],
        compiler_params=pltpu.CompilerParams(vmem_limit_bytes=2 * 1024 * 1024),
    )(*results)


def solution(mesh):
    return jax.shard_map(
        local,
        mesh=mesh,
        in_specs=(
            P("ctx", "head"),
            P("ctx", None),
            P("ctx", None),
            P("ctx", "head"),
            P(),
            P("ctx"),
        ),
        out_specs=(
            P("ctx", "head"),
            P("ctx", "head"),
            P(("ctx", "head"), None),
            P(("ctx", "head"), None),
        ),
        check_vma=False,
    )
```
